32 devices in a mesh: row: 8 (over z, x), col: 4 (over y, core).
Axes of the slice: x: 2, y: 2, z: 4, core: 2. Of those that a mesh axis runs over, the one named last changes fastest.
Arguments:
- patches: bfloat16 [256, 64, 768], P('row', 'col'), may hold values from -6 to 6
- norm_gain: float32 [768], replicated, may hold values from 0.25 to 1.75
- w_qkv: bfloat16 [768, 2304], replicated, may hold values from -0.21875 to 0.21875
- pool_q: float32 [9, 768], replicated, may hold values from -30 to 30, as said below
- pool_kv: float32 [9, 1536], replicated, may hold values from -2 to 2
- w_out: bfloat16 [768, 768], replicated, may hold values from -0.21875 to 0.21875
Outputs:
- mixed: bfloat16 [128, 32, 768], P('row', 'col')
The draws below stay inside these ranges and needn't reach their ends.
Inputs may be any that keep to these rules, and one draw needn't show every extreme that they name: `pool_q`: query pooling taps, nonzero, of either sign.
All inputs are finite; a program needn't handle non-finite values.
Results may differ from the reference program's by a relative error of at most 0.017.
The reference program's roundings to bfloat16 on the way (of `normed`, `projected`, `queries`, `keyvals`, `weights` and `attended`) count: a program that leaves them out, or rounds other values in their place, can miss the bound.
Values may be sent and summed in bfloat16 or wider, within the bound.
A program may use at most 128 MiB of HBM per device.

```python
import math
import jax
import jax.numpy as jnp
from jax import lax

D = 768
HEADS = 12
HEAD = 64
ROWS = 256
COLS = 64
NQ = 4096


def draw_pool_q(key, part):
    sign_key = jax.random.fold_in(key, 11)
    size_key = jax.random.fold_in(key, 12)
    signs = jnp.where(jax.random.bernoulli(sign_key, 0.5, (9, D)), 1.0, -1.0)
    magnitude = jnp.exp(jax.random.uniform(size_key, (9, D), jnp.float32, math.log(0.1), math.log(0.6)))
    return (signs * magnitude).astype(jnp.float32)


def steps_of(stream_key, shape, pieces, smallest, top_value):
    def one(dim, blocks):
        heights = jax.random.uniform(jax.random.fold_in(jax.random.fold_in(stream_key, 6), dim), (blocks,), jnp.float32, smallest / len(pieces), top_value / len(pieces))
        return jnp.repeat(jnp.exp(heights), shape[dim] // blocks).reshape((-1,) + (1,) * (len(shape) - dim - 1))

    factor_of = one(*pieces[0])
    for cut in pieces[1:]:
        factor_of = factor_of * one(*cut)
    return factor_of


def gaussian(key, extent, deviation, bound, pieces=(), dtype=jnp.bfloat16):
    entries = deviation * jax.random.normal(key, extent, jnp.float32)
    if pieces:
        entries = entries * steps_of(key, extent, pieces, -0.22, 0.18)
    return jnp.clip(entries, -bound, bound).astype(dtype)


def setup_inputs(seed: int = 0) -> dict:
    splits = jax.random.split(jax.random.key(seed), 7)
    return {
        "patches": gaussian(splits[0], (ROWS, COLS, D), 1.0, 6.0, ((0, 8), (1, 4))),
        "norm_gain": jnp.clip(1.0 + 0.15 * jax.random.normal(splits[1], (D,), jnp.float32), 0.25, 1.75),
        "w_qkv": gaussian(splits[2], (D, 3 * D), D ** -0.5, 0.21875),
        "pool_q": draw_pool_q(jax.random.fold_in(splits[6], 71), 0),
        "pool_kv": gaussian(splits[4], (9, 2 * D), 0.35, 2.0, (), jnp.float32),
        "w_out": gaussian(splits[5], (D, D), D ** -0.5, 0.21875),
    }


def layer_norm(patches, norm_gain):
    values = patches.astype(jnp.float32)
    center = values - lax.optimization_barrier(jnp.mean(values, axis=-1, keepdims=True))
    spread = lax.optimization_barrier(jnp.mean(center * center, axis=-1, keepdims=True))
    return (center * lax.rsqrt(spread + 1e-06) * norm_gain).astype(jnp.bfloat16)

def pool_grid(padded, kernel, stride, out_rows, out_cols):
    summed = jnp.zeros((out_rows, out_cols, padded.shape[-1]), jnp.float32)
    for row_off in range(3):
        for col_off in range(3):
            window = padded[row_off:row_off + stride * out_rows:stride, col_off:col_off + stride * out_cols:stride]
            summed = summed + kernel[3 * row_off + col_off] * window.astype(jnp.float32)
    return summed.astype(jnp.bfloat16)

def reference(patches, norm_gain, w_qkv, pool_q, pool_kv, w_out):
    normed = layer_norm(patches, norm_gain)
    projected = jnp.dot(normed.reshape(-1, D), w_qkv, preferred_element_type=jnp.float32)
    projected = projected.astype(jnp.bfloat16).reshape(ROWS, COLS, 3 * D)
    padded = jnp.pad(projected, ((1, 0), (1, 0), (0, 0)))
    queries = pool_grid(padded[..., :D], pool_q, 2, ROWS // 2, COLS // 2).reshape(-1, HEADS, HEAD)
    keyvals = pool_grid(padded[..., D:], pool_kv, 4, ROWS // 4, COLS // 4).reshape(-1, 2 * D)
    key_heads = keyvals[:, :D].reshape(-1, HEADS, HEAD).astype(jnp.float32)
    val_heads = keyvals[:, D:].reshape(-1, HEADS, HEAD).astype(jnp.float32)
    scale = float(HEAD) ** (-0.5)
    q_block = math.gcd(512, NQ)
    blocks = queries.reshape(NQ // q_block, q_block, HEADS, HEAD)

    def attend(block):
        scores = jnp.einsum('qhd,khd->hqk', block.astype(jnp.float32), key_heads) * scale
        row_max = lax.optimization_barrier(jnp.max(scores, axis=-1))
        expo = jnp.exp(scores - row_max[..., None])
        total = lax.optimization_barrier(jnp.sum(expo, axis=-1))
        weights = expo.astype(jnp.bfloat16).astype(jnp.float32)
        numer = jnp.einsum('hqk,khd->hqd', weights, val_heads)
        result = numer / total[..., None]
        return result.transpose(1, 0, 2).reshape(q_block, D).astype(jnp.bfloat16)
    attended = lax.map(attend, blocks).reshape(NQ, D)
    mixed = jnp.dot(attended, w_out, preferred_element_type=jnp.float32).astype(jnp.bfloat16)
    return mixed.reshape(ROWS // 2, COLS // 2, D)
```

```python
import functools
import math

import jax
import jax.numpy as jnp
from jax import lax
from jax.experimental import pallas as pl
from jax.experimental.pallas import tpu as pltpu
from jax.sharding import PartitionSpec as P

HEADS = 12
MESH = pl.DeviceIdType.MESH


def passed_along(block, axis, distance):
    devices = range(lax.axis_size(axis))
    route = [(i - distance, i) for i in devices if i - distance in devices]
    return lax.ppermute(block, axis, route)


def layer_norm(patches, norm_gain):
    values = patches.astype(jnp.float32)
    center = values - jnp.mean(values, axis=-1, keepdims=True)
    spread = jnp.mean(center * center, axis=-1, keepdims=True)
    return (center * lax.rsqrt(spread + 1e-06) * norm_gain).astype(jnp.bfloat16)


def pool_grid(padded, kernel, stride, out_rows, out_cols):
    summed = jnp.zeros((out_rows, out_cols, padded.shape[-1]), jnp.float32)
    for row_off in range(3):
        for col_off in range(3):
            window = padded[
                row_off : row_off + stride * out_rows : stride,
                col_off : col_off + stride * out_cols : stride,
            ]
            summed = summed + kernel[3 * row_off + col_off] * window.astype(jnp.float32)
    return summed.astype(jnp.bfloat16)


def make_step(queries, width):
    head_size = width // HEADS
    scale = float(head_size) ** (-0.5)

    def one_block(carry, block):
        run_max, run_sum, accum = carry
        count = block.shape[0]
        key_heads = block[:, :width].reshape(count, HEADS, head_size)
        val_heads = block[:, width:].reshape(count, HEADS, head_size)
        scores = (
            jnp.einsum("qhd,khd->hqk", queries, key_heads, preferred_element_type=jnp.float32)
            * scale
        )
        new_max = jnp.maximum(run_max, jnp.max(scores, axis=-1))
        factor = jnp.exp(run_max - new_max)
        expo = jnp.exp(scores - new_max[..., None])
        run_sum = run_sum * factor + jnp.sum(expo, axis=-1)
        weights = expo.astype(jnp.bfloat16)
        accum = accum * factor[..., None] + jnp.einsum(
            "hqk,khd->hqd", weights, val_heads, preferred_element_type=jnp.float32
        )
        return ((new_max, run_sum, accum), None)

    return one_block


def start_state(query_count, width):
    return (
        jnp.full((HEADS, query_count), -1e30, jnp.float32),
        jnp.zeros((HEADS, query_count), jnp.float32),
        jnp.zeros((HEADS, query_count, width // HEADS), jnp.float32),
    )


def fold_keys(carry, queries, keyvals, width):
    count = keyvals.shape[0]
    block_len = 512
    stacked = keyvals.reshape(count // block_len, block_len, keyvals.shape[1])
    carry, unused = lax.scan(make_step(queries, width), carry, stacked)
    return carry


def on_device(patches, norm_gain, w_qkv, pool_q, pool_kv, w_out):
    tile_rows, tile_cols, width = patches.shape
    head_size = width // HEADS
    normed = layer_norm(patches, norm_gain)
    projected = jnp.dot(normed.reshape(-1, width), w_qkv, preferred_element_type=jnp.float32)
    projected = projected.astype(jnp.bfloat16).reshape(tile_rows, tile_cols, 3 * width)
    upper = passed_along(projected[-1:], "row", 1)
    taller = jnp.concatenate([upper, projected], axis=0)
    left_rim = passed_along(taller[:, -1:], "col", 1)
    extended = jnp.concatenate([left_rim, taller], axis=1)
    query_flat = pool_grid(extended[..., :width], pool_q, 2, tile_rows // 2, tile_cols // 2)
    query_flat = query_flat.reshape(-1, width)
    keyvals = pool_grid(extended[..., width:], pool_kv, 4, tile_rows // 4, tile_cols // 4)
    keyvals = keyvals.reshape(-1, 2 * width)
    query_count = query_flat.shape[0]
    queries = query_flat.reshape(query_count, HEADS, head_size)
    every_key = lax.all_gather(keyvals, ("row", "col"), axis=0, tiled=True)
    carry = fold_keys(start_state(query_count, width), queries, every_key, width)
    run_max, run_sum, accum = carry
    attended = (
        (accum / run_sum[..., None])
        .transpose(1, 0, 2)
        .reshape(query_count, width)
        .astype(jnp.bfloat16)
    )
    mixed = jnp.dot(attended, w_out, preferred_element_type=jnp.float32).astype(jnp.bfloat16)
    return mixed.reshape(tile_rows // 2, tile_cols // 2, width)


def phase_lists():
    kv = [(a - 1, b - 1) for a in range(3) for b in range(3)]
    rest = [(r, c) for r in range(-1, 4) for c in range(-1, 4) if (r, c) not in kv]
    return kv, rest


def select_rows(phases, rows, cols, total, left_at, up_at, corner_at):
    kr, kc = rows // 4, cols // 4
    t = lax.broadcasted_iota(jnp.int32, (kr * kc, 1), 0)
    m = t // kc
    n = t - m * kc
    lanes = lax.broadcasted_iota(jnp.int32, (kr * kc, total), 1)
    parts = []
    for r_off, c_off in phases:
        r, c = 4 * m + r_off, 4 * n + c_off
        src = r * cols + c
        if c_off < 0:
            src = jnp.where(c < 0, left_at + r, src)
        if r_off < 0:
            src = jnp.where(r < 0, jnp.where(c < 0, corner_at, up_at + c), src)
        parts.append(jnp.where(lanes == src, 1.0, 0.0).astype(jnp.bfloat16))
    return jnp.concatenate(parts, axis=0)


def dot32(a, b):
    return jnp.dot(a, b, preferred_element_type=jnp.float32)


def section_kernel(
    nr, nc, patches, gain, w_qkv, pool_q, pool_kv, w_out, out,
    ext, col_out, col_in, row_in, cor_in, kv_out, kv_all, q_out, q_in, att_out, att_in,
    h_send, h_recv, a_send, a_recv, g_send, g_recv, q_send, q_recv, o_send, o_recv,
):
    rows, cols, width = patches.shape
    head = width // HEADS
    group = width // nc
    heads = HEADS // nc
    per = (rows // 4) * (cols // 4)
    r, c = lax.axis_index("row"), lax.axis_index("col")
    partner = r + 1 - 2 * lax.rem(r, 2)
    steps = nr // 2
    local = rows * cols
    left_at, up_at = local, local + rows
    corner_at = up_at + cols + cols - 1
    total = ext.shape[0]

    def peer(k):
        return lax.rem(c + k, nc)

    barrier = pltpu.get_barrier_semaphore()

    def greet(to):
        pl.semaphore_signal(barrier, inc=1, device_id=to, device_id_type=MESH)

    for k in range(1, nc):
        greet((r, peer(k)))
    pl.when(r > 0)(lambda: greet((r - 1, c)))
    pl.when(r < nr - 1)(lambda: greet((r + 1, c)))
    pl.when((r > 0) & (c > 0))(lambda: greet((r - 1, c - 1)))
    pl.when((r < nr - 1) & (c < nc - 1))(lambda: greet((r + 1, c + 1)))
    pl.when(r > 1)(lambda: greet((r - 2, c)))
    pl.when(r < nr - 2)(lambda: greet((r + 2, c)))

    for i in range(rows // 8):
        col_out[8 * i : 8 * i + 8] = patches[8 * i : 8 * i + 8, cols - 1, :]

    def one_if(yes):
        return jnp.where(yes, 1, 0)

    greeters = nc - 1 + one_if(r > 0) + one_if(r < nr - 1) + one_if(r > 1) + one_if(r < nr - 2)
    greeters += one_if((r > 0) & (c > 0)) + one_if((r < nr - 1) & (c < nc - 1))
    pl.semaphore_wait(barrier, greeters)

    def remote(src, dst, send, recv, to):
        return pltpu.make_async_remote_copy(
            src_ref=src, dst_ref=dst, send_sem=send, recv_sem=recv,
            device_id=to, device_id_type=MESH,
        )

    row_copy = remote(patches.at[rows - 1], row_in, h_send.at[0], h_recv.at[0], (r + 1, c))
    col_copy = remote(col_out, col_in, h_send.at[1], h_recv.at[1], (r, c + 1))
    cor_copy = remote(patches.at[rows - 1], cor_in, h_send.at[2], h_recv.at[2], (r + 1, c + 1))
    pl.when(r < nr - 1)(lambda: row_copy.start())
    pl.when(c < nc - 1)(lambda: col_copy.start())
    pl.when((r < nr - 1) & (c < nc - 1))(lambda: cor_copy.start())

    def norm(block):
        values = block.astype(jnp.float32)
        center = values - jnp.mean(values, axis=-1, keepdims=True)
        spread = jnp.mean(center * center, axis=-1, keepdims=True)
        return (center * lax.rsqrt(spread + 1e-06) * gain[...]).astype(jnp.bfloat16)

    piece = 4

    def norm_step(i, carry):
        block = patches[pl.ds(i * piece, piece)].reshape(piece * cols, width)
        at = pl.multiple_of(i * piece * cols, piece * cols)
        ext[pl.ds(at, piece * cols), :] = norm(block)
        return carry

    lax.fori_loop(0, rows // piece, norm_step, 0)

    def halo(present, copy, source, at, count):
        @pl.when(present)
        def _():
            copy.wait_recv()
            ext[at : at + count, :] = norm(source[...])

        @pl.when(jnp.logical_not(present))
        def _():
            ext[at : at + count, :] = jnp.zeros((count, width), jnp.bfloat16)

    halo(r > 0, row_copy, row_in, up_at, cols)
    halo(c > 0, col_copy, col_in, left_at, rows)
    halo((r > 0) & (c > 0), cor_copy, cor_in, up_at + cols, cols)

    kv_phases, rest = phase_lists()
    place = (rows, cols, total, left_at, up_at, corner_at)
    x_kv = dot32(select_rows(kv_phases, *place), ext[...]).astype(jnp.bfloat16)

    def pooled(values, lookup, taps, lanes, base_r, base_c):
        acc = None
        for a in range(3):
            for b in range(3):
                k = lookup[(base_r + a - 1, base_c + b - 1)]
                tap = taps[3 * a + b : 3 * a + b + 1, lanes]
                term = tap * values[k * per : (k + 1) * per].astype(jnp.float32)
                acc = term if acc is None else acc + term
        return acc.astype(jnp.bfloat16)

    kv_at = {p: i for i, p in enumerate(kv_phases)}
    for half in range(2):
        lanes = slice(half * width, (half + 1) * width)
        proj = dot32(x_kv, w_qkv[:, (1 + half) * width : (2 + half) * width]).astype(jnp.bfloat16)
        got = pooled(proj, kv_at, pool_kv, lanes, 0, 0)
        for g in range(nc):
            kv_out[g, :, half * group : (half + 1) * group] = got[:, g * group : (g + 1) * group]

    def kv_copy(k):
        to = peer(k)
        return remote(kv_out.at[to], kv_all.at[r, c], a_send.at[k], a_recv.at[k], (r, to))

    kv_copies = [kv_copy(k) for k in range(1, nc)]
    for copy in kv_copies:
        copy.start()
    kv_all[r, c] = kv_out[c]

    x_rest = dot32(select_rows(rest, *place), ext[...]).astype(jnp.bfloat16)
    x_all = jnp.concatenate([x_kv, x_rest], axis=0)
    all_at = {p: i for i, p in enumerate(kv_phases + rest)}

    for copy in kv_copies:
        copy.wait_recv()

    def relay(slot, lane, to):
        return remote(kv_all.at[slot], kv_all.at[slot], g_send.at[lane, slot], g_recv.at[slot], to)

    def send_up(slot, start):
        copy = relay(slot, 0, (r + 2, c))
        pl.when(r + 2 < nr)(lambda: copy.start() if start else copy.wait_send())

    def send_down(slot, start):
        copy = relay(slot, 1, (r - 2, c))
        pl.when(r >= 2)(lambda: copy.start() if start else copy.wait_send())

    def send_over(slot, start):
        copy = relay(slot, 2, (partner, c))
        copy.start() if start else copy.wait_send()

    def each(step, start):
        low, high = r - 2 * step, r + 2 * step

        @pl.when(low >= 0)
        def _():
            if start:
                relay(low, 0, (r, c)).wait_recv()
            send_up(low, start)
            send_over(low, start)

        @pl.when(high < nr)
        def _():
            if start:
                relay(high, 0, (r, c)).wait_recv()
            send_down(high, start)
            send_over(high, start)

    send_up(r, True)
    send_down(r, True)
    send_over(r, True)

    proj = dot32(x_all, w_qkv[:, :width]).astype(jnp.bfloat16)
    parts = [
        pooled(proj, all_at, pool_q, slice(0, width), 2 * p, 2 * q)
        for p in range(2)
        for q in range(2)
    ]
    mixed_order = jnp.concatenate(parts, axis=0)
    count = 4 * per
    t = lax.broadcasted_iota(jnp.int32, (count, 1), 0)
    q_row = t // (cols // 2)
    q_col = t - q_row * (cols // 2)
    which = 2 * lax.rem(q_row, 2) + lax.rem(q_col, 2)
    src = which * per + (q_row // 2) * (cols // 4) + q_col // 2
    lanes = lax.broadcasted_iota(jnp.int32, (count, count), 1)
    order = jnp.where(lanes == src, 1.0, 0.0).astype(jnp.bfloat16)
    natural = dot32(order, mixed_order).astype(jnp.bfloat16)
    wide = q_out.shape[2]
    for g in range(nc):
        piece_q = natural[:, g * group : (g + 1) * group]
        q_out[g] = jnp.concatenate(
            [piece_q, jnp.zeros((count, wide - group), jnp.bfloat16)], axis=1
        )

    def q_copy(k):
        to = peer(k)
        return remote(q_out.at[to], q_in.at[c], q_send.at[k], q_recv.at[k], (r, to))

    q_copies = [q_copy(k) for k in range(1, nc)]
    for copy in q_copies:
        copy.start()
    q_in[c] = q_out[c]

    for step in range(1, steps):
        each(step, True)
    for copy in q_copies:
        copy.wait_recv()
    for k in range(steps):
        slot = 2 * k + 1 - lax.rem(r, 2)
        relay(slot, 2, (partner, c)).wait_recv()

    keys = nr * nc * per
    factor = float(head) ** (-0.5) * math.log2(math.e)
    kv_lanes = 2 * group

    def attend(g):
        q = q_in[g]
        lane = lax.broadcasted_iota(jnp.int32, (count, wide), 1)
        stacked = jnp.concatenate(
            [
                jnp.where((lane >= h * head) & (lane < (h + 1) * head), q, jnp.zeros_like(q))
                for h in range(heads)
            ],
            axis=0,
        )
        k_part = kv_all[:, :, :, 0:wide].reshape(keys, wide)
        scores = lax.dot_general(
            stacked, k_part, (((1,), (1,)), ((), ())), preferred_element_type=jnp.float32
        )
        top = jnp.max(scores, axis=-1, keepdims=True)
        expo = jnp.exp2((scores - top) * factor)
        summed = jnp.sum(expo, axis=-1, keepdims=True)
        v_part = kv_all[:, :, :, kv_lanes - wide : kv_lanes].reshape(keys, wide)
        numer = dot32(expo.astype(jnp.bfloat16), v_part) / summed
        shift = wide - group
        result = jnp.zeros((count, wide), jnp.float32)
        for h in range(heads):
            inside = (lane >= shift + h * head) & (lane < shift + (h + 1) * head)
            result = jnp.where(inside, numer[h * count : (h + 1) * count], result)
        att_out[g] = result.astype(jnp.bfloat16)

    def att_copy(k):
        to = peer(k)
        return remote(att_out.at[to], att_in.at[c], o_send.at[k], o_recv.at[k], (r, to))

    att_copies = [att_copy(k) for k in range(1, nc)]

    def attend_step(k, carry):
        attend(peer(k + 1))
        return carry

    lax.fori_loop(0, nc - 1, attend_step, 0)
    for copy in att_copies:
        copy.start()
    attend(c)
    att_in[c] = att_out[c]
    for copy in att_copies:
        copy.wait_recv()
    attended = jnp.concatenate([att_in[g][:, wide - group :] for g in range(nc)], axis=1)
    out[...] = dot32(attended, w_out[...]).astype(jnp.bfloat16)

    pl.when(r < nr - 1)(lambda: row_copy.wait_send())
    pl.when(c < nc - 1)(lambda: col_copy.wait_send())
    pl.when((r < nr - 1) & (c < nc - 1))(lambda: cor_copy.wait_send())
    for copy in kv_copies + q_copies + att_copies:
        copy.wait_send()
    send_up(r, False)
    send_down(r, False)
    send_over(r, False)
    for step in range(1, steps):
        each(step, False)


def by_kernel(nr, nc, patches, norm_gain, w_qkv, pool_q, pool_kv, w_out):
    rows, cols, width = patches.shape
    per = (rows // 4) * (cols // 4)
    count = 4 * per
    group = width // nc
    wide = -(-group // 128) * 128
    total = rows * cols + rows + 2 * cols
    total = -(-total // 16) * 16
    bf16 = jnp.bfloat16
    dma = pltpu.SemaphoreType.DMA
    vmem = pl.BlockSpec(memory_space=pltpu.VMEM)
    mixed = pl.pallas_call(
        functools.partial(section_kernel, nr, nc),
        out_shape=jax.ShapeDtypeStruct((count, width), bf16),
        in_specs=[vmem] * 6,
        out_specs=vmem,
        scratch_shapes=[
            pltpu.VMEM((total, width), bf16),
            pltpu.VMEM((rows, width), bf16),
            pltpu.VMEM((rows, width), bf16),
            pltpu.VMEM((cols, width), bf16),
            pltpu.VMEM((cols, width), bf16),
            pltpu.VMEM((nc, per, 2 * group), bf16),
            pltpu.VMEM((nr, nc, per, 2 * group), bf16),
            pltpu.VMEM((nc, count, wide), bf16),
            pltpu.VMEM((nc, count, wide), bf16),
            pltpu.VMEM((nc, count, wide), bf16),
            pltpu.VMEM((nc, count, wide), bf16),
            dma((3,)), dma((3,)),
            dma((nc,)), dma((nc,)),
            dma((3, nr)), dma((nr,)),
            dma((nc,)), dma((nc,)),
            dma((nc,)), dma((nc,)),
        ],
        compiler_params=pltpu.CompilerParams(
            collective_id=0, has_side_effects=True, vmem_limit_bytes=56 * 1024 * 1024
        ),
    )(patches, norm_gain.reshape(1, width), w_qkv, pool_q, pool_kv, w_out)
    return mixed.reshape(rows // 2, cols // 2, width)


def solution(mesh):
    nr, nc = mesh.shape["row"], mesh.shape["col"]
    placed = (P("row", "col", None), P(), P(), P(), P(), P())
    fits = nr % 2 == 0 and HEADS % nc == 0
    body = functools.partial(by_kernel, nr, nc) if fits else on_device
    return jax.shard_map(
        body, mesh=mesh, in_specs=placed, out_specs=P("row", "col", None), check_vma=False
    )
```

```python
import functools
import math

import jax
import jax.numpy as jnp
from jax import lax
from jax.experimental import pallas as pl
from jax.experimental.pallas import tpu as pltpu
from jax.sharding import PartitionSpec as P

HEADS = 12
MESH = pl.DeviceIdType.MESH


def passed_along(block, axis, distance):
    devices = range(lax.axis_size(axis))
    route = [(i - distance, i) for i in devices if i - distance in devices]
    return lax.ppermute(block, axis, route)


def layer_norm(patches, norm_gain):
    values = patches.astype(jnp.float32)
    center = values - jnp.mean(values, axis=-1, keepdims=True)
    spread = jnp.mean(center * center, axis=-1, keepdims=True)
    return (center * lax.rsqrt(spread + 1e-06) * norm_gain).astype(jnp.bfloat16)


def pool_grid(padded, kernel, stride, out_rows, out_cols):
    summed = jnp.zeros((out_rows, out_cols, padded.shape[-1]), jnp.float32)
    for row_off in range(3):
        for col_off in range(3):
            window = padded[
                row_off : row_off + stride * out_rows : stride,
                col_off : col_off + stride * out_cols : stride,
            ]
            summed = summed + kernel[3 * row_off + col_off] * window.astype(jnp.float32)
    return summed.astype(jnp.bfloat16)


def make_step(queries, width):
    head_size = width // HEADS
    scale = float(head_size) ** (-0.5)

    def one_block(carry, block):
        run_max, run_sum, accum = carry
        count = block.shape[0]
        key_heads = block[:, :width].reshape(count, HEADS, head_size)
        val_heads = block[:, width:].reshape(count, HEADS, head_size)
        scores = (
            jnp.einsum("qhd,khd->hqk", queries, key_heads, preferred_element_type=jnp.float32)
            * scale
        )
        new_max = jnp.maximum(run_max, jnp.max(scores, axis=-1))
        factor = jnp.exp(run_max - new_max)
        expo = jnp.exp(scores - new_max[..., None])
        run_sum = run_sum * factor + jnp.sum(expo, axis=-1)
        weights = expo.astype(jnp.bfloat16)
        accum = accum * factor[..., None] + jnp.einsum(
            "hqk,khd->hqd", weights, val_heads, preferred_element_type=jnp.float32
        )
        return ((new_max, run_sum, accum), None)

    return one_block


def start_state(query_count, width):
    return (
        jnp.full((HEADS, query_count), -1e30, jnp.float32),
        jnp.zeros((HEADS, query_count), jnp.float32),
        jnp.zeros((HEADS, query_count, width // HEADS), jnp.float32),
    )


def fold_keys(carry, queries, keyvals, width):
    count = keyvals.shape[0]
    block_len = 512
    stacked = keyvals.reshape(count // block_len, block_len, keyvals.shape[1])
    carry, unused = lax.scan(make_step(queries, width), carry, stacked)
    return carry


def on_device(patches, norm_gain, w_qkv, pool_q, pool_kv, w_out):
    tile_rows, tile_cols, width = patches.shape
    head_size = width // HEADS
    normed = layer_norm(patches, norm_gain)
    projected = jnp.dot(normed.reshape(-1, width), w_qkv, preferred_element_type=jnp.float32)
    projected = projected.astype(jnp.bfloat16).reshape(tile_rows, tile_cols, 3 * width)
    upper = passed_along(projected[-1:], "row", 1)
    taller = jnp.concatenate([upper, projected], axis=0)
    left_rim = passed_along(taller[:, -1:], "col", 1)
    extended = jnp.concatenate([left_rim, taller], axis=1)
    query_flat = pool_grid(extended[..., :width], pool_q, 2, tile_rows // 2, tile_cols // 2)
    query_flat = query_flat.reshape(-1, width)
    keyvals = pool_grid(extended[..., width:], pool_kv, 4, tile_rows // 4, tile_cols // 4)
    keyvals = keyvals.reshape(-1, 2 * width)
    query_count = query_flat.shape[0]
    queries = query_flat.reshape(query_count, HEADS, head_size)
    every_key = lax.all_gather(keyvals, ("row", "col"), axis=0, tiled=True)
    carry = fold_keys(start_state(query_count, width), queries, every_key, width)
    run_max, run_sum, accum = carry
    attended = (
        (accum / run_sum[..., None])
        .transpose(1, 0, 2)
        .reshape(query_count, width)
        .astype(jnp.bfloat16)
    )
    mixed = jnp.dot(attended, w_out, preferred_element_type=jnp.float32).astype(jnp.bfloat16)
    return mixed.reshape(tile_rows // 2, tile_cols // 2, width)


def phase_lists():
    kv_local = [(r, c) for r in range(2) for c in range(2)]
    local = kv_local + [(r, c) for r in range(4) for c in range(4) if (r, c) not in kv_local]
    kv_halo = [(a, b) for a in range(-1, 2) for b in range(-1, 2) if min(a, b) < 0]
    grid = [(r, c) for r in range(-1, 4) for c in range(-1, 4) if min(r, c) < 0]
    halo = kv_halo + [p for p in grid if p not in kv_halo]
    return local, halo, len(kv_local), len(kv_halo)


def select_rows(phases, rows, cols, total, left_at, up_at, corner_at):
    kr, kc = rows // 4, cols // 4
    t = lax.broadcasted_iota(jnp.int32, (kr * kc, 1), 0)
    m = t // kc
    n = t - m * kc
    lanes = lax.broadcasted_iota(jnp.int32, (kr * kc, total), 1)
    parts = []
    for r_off, c_off in phases:
        r, c = 4 * m + r_off, 4 * n + c_off
        src = r * cols + c
        if c_off < 0:
            src = jnp.where(c < 0, left_at + r, src)
        if r_off < 0:
            src = jnp.where(r < 0, jnp.where(c < 0, corner_at, up_at + c), src)
        parts.append(jnp.where(lanes == src, 1.0, 0.0).astype(jnp.bfloat16))
    return jnp.concatenate(parts, axis=0)


def dot32(a, b):
    return jnp.dot(a, b, preferred_element_type=jnp.float32)


def section_kernel(
    nr, nc, patches, gain, w_hbm, pool_q, pool_kv, out,
    ext, col_out, col_in, row_in, cor_in, kv_out, kv_all, q_out, q_in, att_out, att_in,
    w_qkv, acc, peak, summed,
    w_sem, h_send, h_recv, a_send, a_recv, g_send, g_recv, q_send, q_recv, o_send, o_recv,
):
    rows, cols, width = patches.shape
    head = width // HEADS
    group = width // nc
    heads = HEADS // nc
    per = (rows // 4) * (cols // 4)
    r, c = lax.axis_index("row"), lax.axis_index("col")
    side, z = lax.rem(r, 2), r // 2
    core, chip = lax.rem(c, 2), c // 2
    partner = r + 1 - 2 * side
    steps, pairs = nr // 2, nc // 2
    local = rows * cols
    left_at, up_at = local, local + rows
    corner_at = up_at + cols + cols - 1
    total = ext.shape[0]

    w_copies = [
        pltpu.make_async_copy(
            w_hbm.at[:, i * width : (i + 1) * width],
            w_qkv.at[:, i * width : (i + 1) * width],
            w_sem.at[i],
        )
        for i in range(3)
    ]
    for copy in w_copies:
        copy.start()

    def peer(j):
        return 2 * lax.rem(chip + 1 + j // 2, pairs) + lax.rem(core + 1 + j, 2)

    peers = [peer(j) for j in range(nc - 1)]
    barrier = pltpu.get_barrier_semaphore()

    def greet(to):
        pl.semaphore_signal(barrier, inc=1, device_id=to, device_id_type=MESH)

    for to in peers:
        greet((r, to))
    pl.when(r > 0)(lambda: greet((r - 1, c)))
    pl.when(r < nr - 1)(lambda: greet((r + 1, c)))
    pl.when((r > 0) & (c > 0))(lambda: greet((r - 1, c - 1)))
    pl.when((r < nr - 1) & (c < nc - 1))(lambda: greet((r + 1, c + 1)))
    pl.when(r > 1)(lambda: greet((r - 2, c)))
    pl.when(r < nr - 2)(lambda: greet((r + 2, c)))

    for i in range(rows // 8):
        col_out[8 * i : 8 * i + 8] = patches[8 * i : 8 * i + 8, cols - 1, :]

    weight = gain[...].reshape(1, width)

    def norm(block):
        values = block.astype(jnp.float32)
        center = values - jnp.mean(values, axis=-1, keepdims=True)
        spread = jnp.mean(center * center, axis=-1, keepdims=True)
        return (center * lax.rsqrt(spread + 1e-06) * weight).astype(jnp.bfloat16)

    piece = 4

    def norm_step(i, carry):
        block = patches[pl.ds(i * piece, piece)].reshape(piece * cols, width)
        at = pl.multiple_of(i * piece * cols, piece * cols)
        ext[pl.ds(at, piece * cols), :] = norm(block)
        return carry

    early = rows // piece // 2
    lax.fori_loop(0, early, norm_step, 0)

    def one_if(yes):
        return jnp.where(yes, 1, 0)

    greeters = nc - 1 + one_if(r > 0) + one_if(r < nr - 1) + one_if(r > 1) + one_if(r < nr - 2)
    greeters += one_if((r > 0) & (c > 0)) + one_if((r < nr - 1) & (c < nc - 1))
    pl.semaphore_wait(barrier, greeters)

    def remote(src, dst, send, recv, to):
        return pltpu.make_async_remote_copy(
            src_ref=src, dst_ref=dst, send_sem=send, recv_sem=recv,
            device_id=to, device_id_type=MESH,
        )

    row_copy = remote(patches.at[rows - 1], row_in, h_send.at[0], h_recv.at[0], (r + 1, c))
    col_copy = remote(col_out, col_in, h_send.at[1], h_recv.at[1], (r, c + 1))
    cor_copy = remote(patches.at[rows - 1], cor_in, h_send.at[2], h_recv.at[2], (r + 1, c + 1))
    pl.when((r < nr - 1) & (c < nc - 1))(lambda: cor_copy.start())
    pl.when(r < nr - 1)(lambda: row_copy.start())
    pl.when(c < nc - 1)(lambda: col_copy.start())

    lax.fori_loop(early, rows // piece, norm_step, 0)

    local_phases, halo_phases, n_kv_local, n_kv_halo = phase_lists()
    place = (rows, cols)
    marks = (left_at, up_at, corner_at)
    x_local = dot32(select_rows(local_phases, *place, local, *marks), ext[0:local, :])
    x_local = x_local.astype(jnp.bfloat16)

    def project(x, part):
        lanes = slice(part * width, (part + 1) * width)
        return dot32(x, w_qkv[:, lanes]).astype(jnp.bfloat16)

    w_copies[0].wait()
    q_proj = {0: project(x_local, 0)}
    w_copies[1].wait()
    w_copies[2].wait()
    kv_proj = {(0, half): project(x_local[: n_kv_local * per], 1 + half) for half in range(2)}

    def halo(present, copy, source, at, count):
        @pl.when(present)
        def _():
            copy.wait_recv()
            ext[at : at + count, :] = norm(source[...])

        @pl.when(jnp.logical_not(present))
        def _():
            ext[at : at + count, :] = jnp.zeros((count, width), jnp.bfloat16)

    halo(r > 0, row_copy, row_in, up_at, cols)
    halo(c > 0, col_copy, col_in, left_at, rows)
    halo((r > 0) & (c > 0), cor_copy, cor_in, up_at + cols, cols)

    x_halo = dot32(select_rows(halo_phases, *place, total, *marks), ext[...])
    x_halo = x_halo.astype(jnp.bfloat16)
    for half in range(2):
        kv_proj[1, half] = project(x_halo[: n_kv_halo * per], 1 + half)

    found = {p: (0, i) for i, p in enumerate(local_phases)}
    found.update({p: (1, i) for i, p in enumerate(halo_phases)})

    def pooled(values, taps, lanes, base_r, base_c):
        total_term = None
        for a in range(3):
            for b in range(3):
                which, k = found[base_r + a - 1, base_c + b - 1]
                tap = taps[3 * a + b : 3 * a + b + 1, lanes]
                term = tap * values[which][k * per : (k + 1) * per].astype(jnp.float32)
                total_term = term if total_term is None else total_term + term
        return total_term.astype(jnp.bfloat16)

    for half in range(2):
        lanes = slice(half * width, (half + 1) * width)
        got = pooled({w: kv_proj[w, half] for w in range(2)}, pool_kv, lanes, 0, 0)
        for g in range(nc):
            kv_out[g, :, half * group : (half + 1) * group] = got[:, g * group : (g + 1) * group]

    def kv_copy(j, to):
        mine = kv_all.at[side, z, chip, core]
        return remote(kv_out.at[to], mine, a_send.at[j], a_recv.at[c], (r, to))

    def kv_wait(j, to):
        slot = kv_all.at[side, z, to // 2, lax.rem(to, 2)]
        remote(kv_out.at[to], slot, a_send.at[j], a_recv.at[to], (r, to)).wait_recv()

    kv_copies = [kv_copy(j, to) for j, to in enumerate(peers)]
    for copy in kv_copies:
        copy.start()
    kv_all[side, z, chip, core] = kv_out[c]

    def relay(level, pair, lane, to):
        slot = kv_all.at[side, level, pair]
        return remote(slot, slot, g_send.at[lane, level, pair], g_recv.at[side, level, pair], to)

    def send_along(level, pair, lane, start):
        to_row = (r + 2, r - 2, partner)[lane]
        copy = relay(level, pair, lane, (to_row, c))

        def act():
            copy.start() if start else copy.wait_send()

        if lane == 0:
            pl.when(z + 1 < steps)(act)
        elif lane == 1:
            pl.when(z >= 1)(act)
        else:
            act()

    def chunk(j):
        return lax.rem(chip + j, pairs)

    def own(j, start):
        for lane in range(3):
            send_along(z, chunk(j), lane, start)

    def each(step, j, start):
        for level, there, lane in ((z - step, z - step >= 0, 0), (z + step, z + step < steps, 1)):

            @pl.when(there)
            def _():
                if start:
                    relay(level, chunk(j), lane, (partner, c)).wait_recv()
                send_along(level, chunk(j), lane, start)
                send_along(level, chunk(j), 2, start)

    q_proj[1] = project(x_halo, 0)
    kv_wait(nc - 2, peers[nc - 2])
    own(0, True)

    parts = [
        pooled(q_proj, pool_q, slice(0, width), 2 * p, 2 * q) for p in range(2) for q in range(2)
    ]
    mixed_order = jnp.concatenate(parts, axis=0)
    count = 4 * per
    t = lax.broadcasted_iota(jnp.int32, (count, 1), 0)
    q_row = t // (cols // 2)
    q_col = t - q_row * (cols // 2)
    which = 2 * lax.rem(q_row, 2) + lax.rem(q_col, 2)
    src = which * per + (q_row // 2) * (cols // 4) + q_col // 2
    lanes = lax.broadcasted_iota(jnp.int32, (count, count), 1)
    order = jnp.where(lanes == src, 1.0, 0.0).astype(jnp.bfloat16)
    natural = dot32(order, mixed_order).astype(jnp.bfloat16)
    wide = q_out.shape[2]
    for g in range(nc):
        piece_q = natural[:, g * group : (g + 1) * group]
        q_out[g] = jnp.concatenate(
            [piece_q, jnp.zeros((count, wide - group), jnp.bfloat16)], axis=1
        )

    def q_copy(j, to):
        return remote(q_out.at[to], q_in.at[c], q_send.at[j], q_recv.at[c], (r, to))

    q_copies = [q_copy(j, to) for j, to in enumerate(peers)]
    for copy in q_copies:
        copy.start()
    q_in[c] = q_out[c]

    for j in range(nc - 2):
        kv_wait(j, peers[j])
    for j in range(1, pairs):
        own(j, True)
    for step in range(1, steps):
        for j in range(pairs):
            each(step, j, True)
    for j, to in enumerate(peers):
        remote(q_out.at[to], q_in.at[to], q_send.at[j], q_recv.at[to], (r, to)).wait_recv()

    keys = steps * nc * per
    factor = float(head) ** (-0.5) * math.log2(math.e)
    kv_lanes = 2 * group
    lane = lax.broadcasted_iota(jnp.int32, (count, wide), 1)
    shift = wide - group

    def scores_of(g, from_side):
        q = q_in[g]
        stacked = jnp.concatenate(
            [
                jnp.where((lane >= h * head) & (lane < (h + 1) * head), q, jnp.zeros_like(q))
                for h in range(heads)
            ],
            axis=0,
        )
        k_part = kv_all[from_side, :, :, :, :, 0:wide].reshape(keys, wide)
        return lax.dot_general(
            stacked, k_part, (((1,), (1,)), ((), ())), preferred_element_type=jnp.float32
        )

    def weighted(expo, from_side):
        v_part = kv_all[from_side, :, :, :, :, kv_lanes - wide : kv_lanes].reshape(keys, wide)
        return dot32(expo.astype(jnp.bfloat16), v_part)

    def first_half(g, carry):
        scores = scores_of(g, side)
        top = jnp.max(scores, axis=-1, keepdims=True)
        expo = jnp.exp2((scores - top) * factor)
        peak[g] = top
        summed[g] = jnp.sum(expo, axis=-1, keepdims=True)
        acc[g] = weighted(expo, side)
        return carry

    lax.fori_loop(0, nc, first_half, 0)

    for level in range(steps):
        for pair in range(pairs):
            slot = kv_all.at[1 - side, level, pair]
            remote(
                slot, slot, g_send.at[2, level, pair], g_recv.at[1 - side, level, pair],
                (partner, c),
            ).wait_recv()

    def second_half(g):
        scores = scores_of(g, 1 - side)
        before = peak[g]
        top = jnp.maximum(before, jnp.max(scores, axis=-1, keepdims=True))
        expo = jnp.exp2((scores - top) * factor)
        fade = jnp.exp2((before - top) * factor)
        whole = summed[g] * fade + jnp.sum(expo, axis=-1, keepdims=True)
        numer = (acc[g] * fade + weighted(expo, 1 - side)) / whole
        result = jnp.zeros((count, wide), jnp.float32)
        for h in range(heads):
            inside = (lane >= shift + h * head) & (lane < shift + (h + 1) * head)
            result = jnp.where(inside, numer[h * count : (h + 1) * count], result)
        result = result[:, shift:].astype(jnp.bfloat16)
        half = count // 2
        att_out[g] = jnp.concatenate([result[:half], result[half:]], axis=1)

    def att_copy(j, to):
        return remote(att_out.at[to], att_in.at[c], o_send.at[j], o_recv.at[c], (r, to))

    def second_step(j, carry):
        to = peer(j)
        second_half(to)
        att_copy(j, to).start()
        return carry

    lax.fori_loop(0, nc - 1, second_step, 0)
    second_half(c)
    att_in[c] = att_out[c]
    for j, to in enumerate(peers):
        remote(att_out.at[to], att_in.at[to], o_send.at[j], o_recv.at[to], (r, to)).wait_recv()
    half = count // 2
    out[:half] = jnp.concatenate([att_in[g][:, :group] for g in range(nc)], axis=1)
    out[half:] = jnp.concatenate([att_in[g][:, group:] for g in range(nc)], axis=1)

    pl.when(r < nr - 1)(lambda: row_copy.wait_send())
    pl.when(c < nc - 1)(lambda: col_copy.wait_send())
    pl.when((r < nr - 1) & (c < nc - 1))(lambda: cor_copy.wait_send())
    for copy in kv_copies + q_copies:
        copy.wait_send()
    for j, to in enumerate(peers):
        att_copy(j, to).wait_send()
    for j in range(pairs):
        own(j, False)
    for step in range(1, steps):
        for j in range(pairs):
            each(step, j, False)


def by_kernel(nr, nc, patches, norm_gain, w_qkv, pool_q, pool_kv, w_out):
    rows, cols, width = patches.shape
    per = (rows // 4) * (cols // 4)
    count = 4 * per
    group = width // nc
    heads = HEADS // nc
    wide = -(-group // 128) * 128
    total = rows * cols + rows + 2 * cols
    total = -(-total // 16) * 16
    steps, pairs = nr // 2, nc // 2
    bf16, f32 = jnp.bfloat16, jnp.float32
    dma = pltpu.SemaphoreType.DMA
    vmem = pl.BlockSpec(memory_space=pltpu.VMEM)
    attended = pl.pallas_call(
        functools.partial(section_kernel, nr, nc),
        out_shape=jax.ShapeDtypeStruct((count, width), bf16),
        in_specs=[vmem, vmem, pl.BlockSpec(memory_space=pl.ANY), vmem, vmem],
        out_specs=vmem,
        scratch_shapes=[
            pltpu.VMEM((total, width), bf16),
            pltpu.VMEM((rows, width), bf16),
            pltpu.VMEM((rows, width), bf16),
            pltpu.VMEM((cols, width), bf16),
            pltpu.VMEM((cols, width), bf16),
            pltpu.VMEM((nc, per, 2 * group), bf16),
            pltpu.VMEM((2, steps, pairs, 2, per, 2 * group), bf16),
            pltpu.VMEM((nc, count, wide), bf16),
            pltpu.VMEM((nc, count, wide), bf16),
            pltpu.VMEM((nc, count // 2, 2 * group), bf16),
            pltpu.VMEM((nc, count // 2, 2 * group), bf16),
            pltpu.VMEM(w_qkv.shape, bf16),
            pltpu.VMEM((nc, heads * count, wide), f32),
            pltpu.VMEM((nc, heads * count, 1), f32),
            pltpu.VMEM((nc, heads * count, 1), f32),
            dma((3,)),
            dma((3,)), dma((3,)),
            dma((nc,)), dma((nc,)),
            dma((3, steps, pairs)), dma((2, steps, pairs)),
            dma((nc,)), dma((nc,)),
            dma((nc,)), dma((nc,)),
        ],
        compiler_params=pltpu.CompilerParams(
            collective_id=0, has_side_effects=True, vmem_limit_bytes=56 * 1024 * 1024
        ),
    )(patches, norm_gain, w_qkv, pool_q, pool_kv)
    mixed = jnp.dot(attended, w_out, preferred_element_type=f32).astype(bf16)
    return mixed.reshape(rows // 2, cols // 2, width)


def solution(mesh):
    nr, nc = mesh.shape["row"], mesh.shape["col"]
    placed = (P("row", "col", None), P(), P(), P(), P(), P())
    fits = nr % 2 == 0 and nc % 2 == 0 and HEADS % nc == 0
    body = functools.partial(by_kernel, nr, nc) if fits else on_device
    return jax.shard_map(
        body, mesh=mesh, in_specs=placed, out_specs=P("row", "col", None), check_vma=False
    )
```

```python
import functools
import math

import jax
import jax.numpy as jnp
from jax import lax
from jax.experimental import pallas as pl
from jax.experimental.pallas import tpu as pltpu
from jax.sharding import PartitionSpec as P

HEADS = 12
MESH = pl.DeviceIdType.MESH


def passed_along(block, axis, distance):
    devices = range(lax.axis_size(axis))
    route = [(i - distance, i) for i in devices if i - distance in devices]
    return lax.ppermute(block, axis, route)


def layer_norm(patches, norm_gain):
    values = patches.astype(jnp.float32)
    center = values - jnp.mean(values, axis=-1, keepdims=True)
    spread = jnp.mean(center * center, axis=-1, keepdims=True)
    return (center * lax.rsqrt(spread + 1e-06) * norm_gain).astype(jnp.bfloat16)


def pool_grid(padded, kernel, stride, out_rows, out_cols):
    summed = jnp.zeros((out_rows, out_cols, padded.shape[-1]), jnp.float32)
    for row_off in range(3):
        for col_off in range(3):
            window = padded[
                row_off : row_off + stride * out_rows : stride,
                col_off : col_off + stride * out_cols : stride,
            ]
            summed = summed + kernel[3 * row_off + col_off] * window.astype(jnp.float32)
    return summed.astype(jnp.bfloat16)


def make_step(queries, width):
    head_size = width // HEADS
    scale = float(head_size) ** (-0.5)

    def one_block(carry, block):
        run_max, run_sum, accum = carry
        count = block.shape[0]
        key_heads = block[:, :width].reshape(count, HEADS, head_size)
        val_heads = block[:, width:].reshape(count, HEADS, head_size)
        scores = (
            jnp.einsum("qhd,khd->hqk", queries, key_heads, preferred_element_type=jnp.float32)
            * scale
        )
        new_max = jnp.maximum(run_max, jnp.max(scores, axis=-1))
        factor = jnp.exp(run_max - new_max)
        expo = jnp.exp(scores - new_max[..., None])
        run_sum = run_sum * factor + jnp.sum(expo, axis=-1)
        weights = expo.astype(jnp.bfloat16)
        accum = accum * factor[..., None] + jnp.einsum(
            "hqk,khd->hqd", weights, val_heads, preferred_element_type=jnp.float32
        )
        return ((new_max, run_sum, accum), None)

    return one_block


def start_state(query_count, width):
    return (
        jnp.full((HEADS, query_count), -1e30, jnp.float32),
        jnp.zeros((HEADS, query_count), jnp.float32),
        jnp.zeros((HEADS, query_count, width // HEADS), jnp.float32),
    )


def fold_keys(carry, queries, keyvals, width):
    count = keyvals.shape[0]
    block_len = 512
    stacked = keyvals.reshape(count // block_len, block_len, keyvals.shape[1])
    carry, unused = lax.scan(make_step(queries, width), carry, stacked)
    return carry


def on_device(patches, norm_gain, w_qkv, pool_q, pool_kv, w_out):
    tile_rows, tile_cols, width = patches.shape
    head_size = width // HEADS
    normed = layer_norm(patches, norm_gain)
    projected = jnp.dot(normed.reshape(-1, width), w_qkv, preferred_element_type=jnp.float32)
    projected = projected.astype(jnp.bfloat16).reshape(tile_rows, tile_cols, 3 * width)
    upper = passed_along(projected[-1:], "row", 1)
    taller = jnp.concatenate([upper, projected], axis=0)
    left_rim = passed_along(taller[:, -1:], "col", 1)
    extended = jnp.concatenate([left_rim, taller], axis=1)
    query_flat = pool_grid(extended[..., :width], pool_q, 2, tile_rows // 2, tile_cols // 2)
    query_flat = query_flat.reshape(-1, width)
    keyvals = pool_grid(extended[..., width:], pool_kv, 4, tile_rows // 4, tile_cols // 4)
    keyvals = keyvals.reshape(-1, 2 * width)
    query_count = query_flat.shape[0]
    queries = query_flat.reshape(query_count, HEADS, head_size)
    every_key = lax.all_gather(keyvals, ("row", "col"), axis=0, tiled=True)
    carry = fold_keys(start_state(query_count, width), queries, every_key, width)
    run_max, run_sum, accum = carry
    attended = (
        (accum / run_sum[..., None])
        .transpose(1, 0, 2)
        .reshape(query_count, width)
        .astype(jnp.bfloat16)
    )
    mixed = jnp.dot(attended, w_out, preferred_element_type=jnp.float32).astype(jnp.bfloat16)
    return mixed.reshape(tile_rows // 2, tile_cols // 2, width)


def phase_lists():
    kv_local = [(r, c) for r in range(2) for c in range(2)]
    local = kv_local + [(r, c) for r in range(4) for c in range(4) if (r, c) not in kv_local]
    kv_halo = [(a, b) for a in range(-1, 2) for b in range(-1, 2) if min(a, b) < 0]
    grid = [(r, c) for r in range(-1, 4) for c in range(-1, 4) if min(r, c) < 0]
    halo = kv_halo + [p for p in grid if p not in kv_halo]
    return local, halo, len(kv_local), len(kv_halo)


def select_rows(phases, rows, cols, total, left_at, up_at, corner_at):
    kr, kc = rows // 4, cols // 4
    t = lax.broadcasted_iota(jnp.int32, (kr * kc, 1), 0)
    m = t // kc
    n = t - m * kc
    lanes = lax.broadcasted_iota(jnp.int32, (kr * kc, total), 1)
    parts = []
    for r_off, c_off in phases:
        r, c = 4 * m + r_off, 4 * n + c_off
        src = r * cols + c
        if c_off < 0:
            src = jnp.where(c < 0, left_at + r, src)
        if r_off < 0:
            src = jnp.where(r < 0, jnp.where(c < 0, corner_at, up_at + c), src)
        parts.append(jnp.where(lanes == src, 1.0, 0.0).astype(jnp.bfloat16))
    return jnp.concatenate(parts, axis=0)


def dot32(a, b):
    return jnp.dot(a, b, preferred_element_type=jnp.float32)


def section_kernel(
    nr, nc, patches, gain, w_hbm, pool_q, pool_kv, out,
    ext, col_out, col_in, row_in, cor_in, kv_out, kv_all, q_out, q_in, att_out, att_in,
    w_qkv, q_all, acc, peak, summed,
    w_sem, h_send, h_recv, a_send, a_recv, g_send, g_recv, q_send, q_recv, o_send, o_recv,
):
    rows, cols, width = patches.shape
    head = width // HEADS
    group = width // nc
    heads = HEADS // nc
    per = (rows // 4) * (cols // 4)
    r, c = lax.axis_index("row"), lax.axis_index("col")
    side, z = lax.rem(r, 2), r // 2
    core, chip = lax.rem(c, 2), c // 2
    partner = r + 1 - 2 * side
    steps, pairs = nr // 2, nc // 2
    local = rows * cols
    left_at, up_at = local, local + rows
    corner_at = up_at + cols + cols - 1
    total = ext.shape[0]

    w_copies = [
        pltpu.make_async_copy(
            w_hbm.at[:, i * width : (i + 1) * width],
            w_qkv.at[:, i * width : (i + 1) * width],
            w_sem.at[i],
        )
        for i in range(3)
    ]
    for copy in w_copies:
        copy.start()

    def peer(j):
        return 2 * lax.rem(chip + 1 + j // 2, pairs) + lax.rem(core + 1 + j, 2)

    peers = [peer(j) for j in range(nc - 1)]
    barrier = pltpu.get_barrier_semaphore()

    def greet(to):
        pl.semaphore_signal(barrier, inc=1, device_id=to, device_id_type=MESH)

    for to in peers:
        greet((r, to))
    pl.when(r > 0)(lambda: greet((r - 1, c)))
    pl.when(r < nr - 1)(lambda: greet((r + 1, c)))
    pl.when((r > 0) & (c > 0))(lambda: greet((r - 1, c - 1)))
    pl.when((r < nr - 1) & (c < nc - 1))(lambda: greet((r + 1, c + 1)))
    pl.when(r > 1)(lambda: greet((r - 2, c)))
    pl.when(r < nr - 2)(lambda: greet((r + 2, c)))

    for i in range(rows // 8):
        col_out[8 * i : 8 * i + 8] = patches[8 * i : 8 * i + 8, cols - 1, :]

    weight = gain[...].reshape(1, width)

    def norm(block):
        values = block.astype(jnp.float32)
        center = values - jnp.mean(values, axis=-1, keepdims=True)
        spread = jnp.mean(center * center, axis=-1, keepdims=True)
        return (center * lax.rsqrt(spread + 1e-06) * weight).astype(jnp.bfloat16)

    piece = 4

    def norm_step(i, carry):
        block = patches[pl.ds(i * piece, piece)].reshape(piece * cols, width)
        at = pl.multiple_of(i * piece * cols, piece * cols)
        ext[pl.ds(at, piece * cols), :] = norm(block)
        return carry

    early = rows // piece // 2
    lax.fori_loop(0, early, norm_step, 0, unroll=True)

    def one_if(yes):
        return jnp.where(yes, 1, 0)

    greeters = nc - 1 + one_if(r > 0) + one_if(r < nr - 1) + one_if(r > 1) + one_if(r < nr - 2)
    greeters += one_if((r > 0) & (c > 0)) + one_if((r < nr - 1) & (c < nc - 1))
    pl.semaphore_wait(barrier, greeters)

    def remote(src, dst, send, recv, to):
        return pltpu.make_async_remote_copy(
            src_ref=src, dst_ref=dst, send_sem=send, recv_sem=recv,
            device_id=to, device_id_type=MESH,
        )

    row_copy = remote(patches.at[rows - 1], row_in, h_send.at[0], h_recv.at[0], (r + 1, c))
    col_copy = remote(col_out, col_in, h_send.at[1], h_recv.at[1], (r, c + 1))
    cor_copy = remote(patches.at[rows - 1], cor_in, h_send.at[2], h_recv.at[2], (r + 1, c + 1))
    pl.when((r < nr - 1) & (c < nc - 1))(lambda: cor_copy.start())
    pl.when(r < nr - 1)(lambda: row_copy.start())
    pl.when(c < nc - 1)(lambda: col_copy.start())

    lax.fori_loop(early, rows // piece, norm_step, 0, unroll=True)

    local_phases, halo_phases, n_kv_local, n_kv_halo = phase_lists()
    place = (rows, cols)
    marks = (left_at, up_at, corner_at)
    x_local = dot32(select_rows(local_phases, *place, local, *marks), ext[0:local, :])
    x_local = x_local.astype(jnp.bfloat16)

    def project(x, part):
        lanes = slice(part * width, (part + 1) * width)
        return dot32(x, w_qkv[:, lanes]).astype(jnp.bfloat16)

    w_copies[0].wait()
    q_proj = {0: project(x_local, 0)}
    w_copies[1].wait()
    w_copies[2].wait()
    kv_proj = {(0, half): project(x_local[: n_kv_local * per], 1 + half) for half in range(2)}

    def halo(present, copy, source, at, count):
        @pl.when(present)
        def _():
            copy.wait_recv()
            ext[at : at + count, :] = norm(source[...])

        @pl.when(jnp.logical_not(present))
        def _():
            ext[at : at + count, :] = jnp.zeros((count, width), jnp.bfloat16)

    halo(r > 0, row_copy, row_in, up_at, cols)
    halo(c > 0, col_copy, col_in, left_at, rows)
    halo((r > 0) & (c > 0), cor_copy, cor_in, up_at + cols, cols)

    x_halo = dot32(select_rows(halo_phases, *place, total, *marks), ext[...])
    x_halo = x_halo.astype(jnp.bfloat16)
    for half in range(2):
        kv_proj[1, half] = project(x_halo[: n_kv_halo * per], 1 + half)

    found = {p: (0, i) for i, p in enumerate(local_phases)}
    found.update({p: (1, i) for i, p in enumerate(halo_phases)})

    def pooled(values, taps, lanes, base_r, base_c):
        total_term = None
        for a in range(3):
            for b in range(3):
                which, k = found[base_r + a - 1, base_c + b - 1]
                tap = taps[3 * a + b : 3 * a + b + 1, lanes]
                term = tap * values[which][k * per : (k + 1) * per].astype(jnp.float32)
                total_term = term if total_term is None else total_term + term
        return total_term.astype(jnp.bfloat16)

    for half in range(2):
        lanes = slice(half * width, (half + 1) * width)
        got = pooled({w: kv_proj[w, half] for w in range(2)}, pool_kv, lanes, 0, 0)
        for g in range(nc):
            kv_out[g, :, half * group : (half + 1) * group] = got[:, g * group : (g + 1) * group]

    def kv_copy(j, to):
        mine = kv_all.at[side, z, chip, core]
        return remote(kv_out.at[to], mine, a_send.at[j], a_recv.at[c], (r, to))

    def kv_wait(j, to):
        slot = kv_all.at[side, z, to // 2, lax.rem(to, 2)]
        remote(kv_out.at[to], slot, a_send.at[j], a_recv.at[to], (r, to)).wait_recv()

    kv_copies = [kv_copy(j, to) for j, to in enumerate(peers)]
    for copy in kv_copies:
        copy.start()
    kv_all[side, z, chip, core] = kv_out[c]

    def relay(level, pair, lane, to):
        slot = kv_all.at[side, level, pair]
        return remote(slot, slot, g_send.at[lane, level, pair], g_recv.at[side, level, pair], to)

    def send_along(level, pair, lane, start):
        to_row = (r + 2, r - 2, partner)[lane]
        copy = relay(level, pair, lane, (to_row, c))

        def act():
            copy.start() if start else copy.wait_send()

        if lane == 0:
            pl.when(z + 1 < steps)(act)
        elif lane == 1:
            pl.when(z >= 1)(act)
        else:
            act()

    def chunk(j):
        return lax.rem(chip + j, pairs)

    def own(j, start):
        for lane in range(3):
            send_along(z, chunk(j), lane, start)

    def each(step, j, start):
        for level, there, lane in ((z - step, z - step >= 0, 0), (z + step, z + step < steps, 1)):

            @pl.when(there)
            def _():
                if start:
                    relay(level, chunk(j), lane, (partner, c)).wait_recv()
                send_along(level, chunk(j), lane, start)
                send_along(level, chunk(j), 2, start)

    q_proj[1] = project(x_halo, 0)
    kv_wait(nc - 2, peers[nc - 2])
    own(0, True)

    parts = [
        pooled(q_proj, pool_q, slice(0, width), 2 * p, 2 * q) for p in range(2) for q in range(2)
    ]
    mixed_order = jnp.concatenate(parts, axis=0)
    count = 4 * per
    t = lax.broadcasted_iota(jnp.int32, (count, 1), 0)
    q_row = t // (cols // 2)
    q_col = t - q_row * (cols // 2)
    which = 2 * lax.rem(q_row, 2) + lax.rem(q_col, 2)
    src = which * per + (q_row // 2) * (cols // 4) + q_col // 2
    lanes = lax.broadcasted_iota(jnp.int32, (count, count), 1)
    order = jnp.where(lanes == src, 1.0, 0.0).astype(jnp.bfloat16)
    natural = dot32(order, mixed_order).astype(jnp.bfloat16)
    wide = q_out.shape[2]
    for g in range(nc):
        piece_q = natural[:, g * group : (g + 1) * group]
        q_out[g] = jnp.concatenate(
            [piece_q, jnp.zeros((count, wide - group), jnp.bfloat16)], axis=1
        )

    def q_copy(j, to):
        return remote(q_out.at[to], q_in.at[c], q_send.at[j], q_recv.at[c], (r, to))

    q_copies = [q_copy(j, to) for j, to in enumerate(peers)]
    for copy in q_copies:
        copy.start()
    q_in[c] = q_out[c]

    for j in range(nc - 2):
        kv_wait(j, peers[j])
    for j in range(1, pairs):
        own(j, True)
    keys = nc * per
    factor = float(head) ** (-0.5) * math.log2(math.e)
    kv_lanes = 2 * group
    lane = lax.broadcasted_iota(jnp.int32, (count, wide), 1)
    shift = wide - group
    stack = heads * count

    def stack_queries():
        for j, to in enumerate(peers):
            remote(q_out.at[to], q_in.at[to], q_send.at[j], q_recv.at[to], (r, to)).wait_recv()
        for g in range(nc):
            q = q_in[g]
            for h in range(heads):
                kept = (lane >= h * head) & (lane < (h + 1) * head)
                at = g * stack + h * count
                q_all[at : at + count, :] = jnp.where(kept, q, jnp.zeros_like(q))

    def absorb(from_side, level, first=False):
        k_part = kv_all[from_side, level, :, :, :, 0:wide].reshape(keys, wide)
        v_part = kv_all[from_side, level, :, :, :, kv_lanes - wide : kv_lanes].reshape(keys, wide)
        scores = lax.dot_general(
            q_all[...], k_part, (((1,), (1,)), ((), ())), preferred_element_type=jnp.float32
        )
        high = jnp.max(scores, axis=-1, keepdims=True)
        top = high if first else jnp.maximum(peak[...], high)
        expo = jnp.exp2((scores - top) * factor)
        piece_sum = jnp.sum(expo, axis=-1, keepdims=True)
        numer = dot32(expo.astype(jnp.bfloat16), v_part)
        if first:
            summed[...] = piece_sum
            acc[...] = numer
        else:
            fade = jnp.exp2((peak[...] - top) * factor)
            summed[...] = summed[...] * fade + piece_sum
            acc[...] = acc[...] * fade + numer
        peak[...] = top

    def absorb_both(step, visit):
        def one(k, carry):
            level = z - step + 2 * k * step
            pl.when((level >= 0) & (level < steps))(lambda: visit(level))
            return carry

        lax.fori_loop(0, 2, one, 0)

    for j in range(pairs):
        each(1, j, True)
    stack_queries()
    absorb(side, z, True)

    def own_step(step, carry):
        absorb_both(step, lambda level: absorb(side, level))
        for j in range(pairs):
            each(step + 1, j, True)
        return carry

    lax.fori_loop(1, steps, own_step, 0)

    def from_partner(level):
        for pair in range(pairs):
            slot = kv_all.at[1 - side, level, pair]
            remote(
                slot, slot, g_send.at[2, level, pair], g_recv.at[1 - side, level, pair],
                (partner, c),
            ).wait_recv()
        absorb(1 - side, level)

    def partner_step(k, carry):
        step = (k + 1) // 2
        level = z + step * (2 * lax.rem(k, 2) - 1)
        pl.when((level >= 0) & (level < steps))(lambda: from_partner(level))
        return carry

    lax.fori_loop(0, 2 * steps - 1, partner_step, 0)

    def finish(g):
        rows_g = pl.ds(pl.multiple_of(g * stack, stack), stack)
        numer = acc[rows_g, :] / summed[rows_g, :]
        result = jnp.zeros((count, wide), jnp.float32)
        for h in range(heads):
            inside = (lane >= shift + h * head) & (lane < shift + (h + 1) * head)
            result = jnp.where(inside, numer[h * count : (h + 1) * count], result)
        result = result[:, shift:].astype(jnp.bfloat16)
        half = count // 2
        att_out[g] = jnp.concatenate([result[:half], result[half:]], axis=1)

    def att_copy(j, to):
        return remote(att_out.at[to], att_in.at[c], o_send.at[j], o_recv.at[c], (r, to))

    def second_step(j, carry):
        to = peer(j)
        finish(to)
        att_copy(j, to).start()
        return carry

    lax.fori_loop(0, nc - 1, second_step, 0)
    finish(c)
    att_in[c] = att_out[c]
    for j, to in enumerate(peers):
        remote(att_out.at[to], att_in.at[to], o_send.at[j], o_recv.at[to], (r, to)).wait_recv()
    half = count // 2
    out[:half] = jnp.concatenate([att_in[g][:, :group] for g in range(nc)], axis=1)
    out[half:] = jnp.concatenate([att_in[g][:, group:] for g in range(nc)], axis=1)

    pl.when(r < nr - 1)(lambda: row_copy.wait_send())
    pl.when(c < nc - 1)(lambda: col_copy.wait_send())
    pl.when((r < nr - 1) & (c < nc - 1))(lambda: cor_copy.wait_send())
    for copy in kv_copies + q_copies:
        copy.wait_send()
    for j, to in enumerate(peers):
        att_copy(j, to).wait_send()
    for j in range(pairs):
        own(j, False)
    for step in range(1, steps):
        for j in range(pairs):
            each(step, j, False)


def by_kernel(nr, nc, patches, norm_gain, w_qkv, pool_q, pool_kv, w_out):
    rows, cols, width = patches.shape
    per = (rows // 4) * (cols // 4)
    count = 4 * per
    group = width // nc
    heads = HEADS // nc
    wide = -(-group // 128) * 128
    total = rows * cols + rows + 2 * cols
    total = -(-total // 16) * 16
    steps, pairs = nr // 2, nc // 2
    bf16, f32 = jnp.bfloat16, jnp.float32
    dma = pltpu.SemaphoreType.DMA
    vmem = pl.BlockSpec(memory_space=pltpu.VMEM)
    attended = pl.pallas_call(
        functools.partial(section_kernel, nr, nc),
        out_shape=jax.ShapeDtypeStruct((count, width), bf16),
        in_specs=[vmem, vmem, pl.BlockSpec(memory_space=pl.ANY), vmem, vmem],
        out_specs=vmem,
        scratch_shapes=[
            pltpu.VMEM((total, width), bf16),
            pltpu.VMEM((rows, width), bf16),
            pltpu.VMEM((rows, width), bf16),
            pltpu.VMEM((cols, width), bf16),
            pltpu.VMEM((cols, width), bf16),
            pltpu.VMEM((nc, per, 2 * group), bf16),
            pltpu.VMEM((2, steps, pairs, 2, per, 2 * group), bf16),
            pltpu.VMEM((nc, count, wide), bf16),
            pltpu.VMEM((nc, count, wide), bf16),
            pltpu.VMEM((nc, count // 2, 2 * group), bf16),
            pltpu.VMEM((nc, count // 2, 2 * group), bf16),
            pltpu.VMEM(w_qkv.shape, bf16),
            pltpu.VMEM((nc * heads * count, wide), bf16),
            pltpu.VMEM((nc * heads * count, wide), f32),
            pltpu.VMEM((nc * heads * count, 1), f32),
            pltpu.VMEM((nc * heads * count, 1), f32),
            dma((3,)),
            dma((3,)), dma((3,)),
            dma((nc,)), dma((nc,)),
            dma((3, steps, pairs)), dma((2, steps, pairs)),
            dma((nc,)), dma((nc,)),
            dma((nc,)), dma((nc,)),
        ],
        compiler_params=pltpu.CompilerParams(
            collective_id=0, has_side_effects=True, vmem_limit_bytes=56 * 1024 * 1024
        ),
    )(patches, norm_gain, w_qkv, pool_q, pool_kv)
    mixed = jnp.dot(attended, w_out, preferred_element_type=f32).astype(bf16)
    return mixed.reshape(rows // 2, cols // 2, width)


def solution(mesh):
    nr, nc = mesh.shape["row"], mesh.shape["col"]
    placed = (P("row", "col", None), P(), P(), P(), P(), P())
    fits = nr % 2 == 0 and nc % 2 == 0 and HEADS % nc == 0
    body = functools.partial(by_kernel, nr, nc) if fits else on_device
    return jax.shard_map(
        body, mesh=mesh, in_specs=placed, out_specs=P("row", "col", None), check_vma=False
    )
```

```python
import functools
import math

import jax
import jax.numpy as jnp
from jax import lax
from jax.experimental import pallas as pl
from jax.experimental.pallas import tpu as pltpu
from jax.sharding import PartitionSpec as P

HEADS = 12
MESH = pl.DeviceIdType.MESH


def passed_along(block, axis, distance):
    devices = range(lax.axis_size(axis))
    route = [(i - distance, i) for i in devices if i - distance in devices]
    return lax.ppermute(block, axis, route)


def layer_norm(patches, norm_gain):
    values = patches.astype(jnp.float32)
    center = values - jnp.mean(values, axis=-1, keepdims=True)
    spread = jnp.mean(center * center, axis=-1, keepdims=True)
    return (center * lax.rsqrt(spread + 1e-06) * norm_gain).astype(jnp.bfloat16)


def pool_grid(padded, kernel, stride, out_rows, out_cols):
    summed = jnp.zeros((out_rows, out_cols, padded.shape[-1]), jnp.float32)
    for row_off in range(3):
        for col_off in range(3):
            window = padded[
                row_off : row_off + stride * out_rows : stride,
                col_off : col_off + stride * out_cols : stride,
            ]
            summed = summed + kernel[3 * row_off + col_off] * window.astype(jnp.float32)
    return summed.astype(jnp.bfloat16)


def make_step(queries, width):
    head_size = width // HEADS
    scale = float(head_size) ** (-0.5)

    def one_block(carry, block):
        run_max, run_sum, accum = carry
        count = block.shape[0]
        key_heads = block[:, :width].reshape(count, HEADS, head_size)
        val_heads = block[:, width:].reshape(count, HEADS, head_size)
        scores = (
            jnp.einsum("qhd,khd->hqk", queries, key_heads, preferred_element_type=jnp.float32)
            * scale
        )
        new_max = jnp.maximum(run_max, jnp.max(scores, axis=-1))
        factor = jnp.exp(run_max - new_max)
        expo = jnp.exp(scores - new_max[..., None])
        run_sum = run_sum * factor + jnp.sum(expo, axis=-1)
        weights = expo.astype(jnp.bfloat16)
        accum = accum * factor[..., None] + jnp.einsum(
            "hqk,khd->hqd", weights, val_heads, preferred_element_type=jnp.float32
        )
        return ((new_max, run_sum, accum), None)

    return one_block


def start_state(query_count, width):
    return (
        jnp.full((HEADS, query_count), -1e30, jnp.float32),
        jnp.zeros((HEADS, query_count), jnp.float32),
        jnp.zeros((HEADS, query_count, width // HEADS), jnp.float32),
    )


def fold_keys(carry, queries, keyvals, width):
    count = keyvals.shape[0]
    block_len = 512
    stacked = keyvals.reshape(count // block_len, block_len, keyvals.shape[1])
    carry, unused = lax.scan(make_step(queries, width), carry, stacked)
    return carry


def on_device(patches, norm_gain, w_qkv, pool_q, pool_kv, w_out):
    tile_rows, tile_cols, width = patches.shape
    head_size = width // HEADS
    normed = layer_norm(patches, norm_gain)
    projected = jnp.dot(normed.reshape(-1, width), w_qkv, preferred_element_type=jnp.float32)
    projected = projected.astype(jnp.bfloat16).reshape(tile_rows, tile_cols, 3 * width)
    upper = passed_along(projected[-1:], "row", 1)
    taller = jnp.concatenate([upper, projected], axis=0)
    left_rim = passed_along(taller[:, -1:], "col", 1)
    extended = jnp.concatenate([left_rim, taller], axis=1)
    query_flat = pool_grid(extended[..., :width], pool_q, 2, tile_rows // 2, tile_cols // 2)
    query_flat = query_flat.reshape(-1, width)
    keyvals = pool_grid(extended[..., width:], pool_kv, 4, tile_rows // 4, tile_cols // 4)
    keyvals = keyvals.reshape(-1, 2 * width)
    query_count = query_flat.shape[0]
    queries = query_flat.reshape(query_count, HEADS, head_size)
    every_key = lax.all_gather(keyvals, ("row", "col"), axis=0, tiled=True)
    carry = fold_keys(start_state(query_count, width), queries, every_key, width)
    run_max, run_sum, accum = carry
    attended = (
        (accum / run_sum[..., None])
        .transpose(1, 0, 2)
        .reshape(query_count, width)
        .astype(jnp.bfloat16)
    )
    mixed = jnp.dot(attended, w_out, preferred_element_type=jnp.float32).astype(jnp.bfloat16)
    return mixed.reshape(tile_rows // 2, tile_cols // 2, width)


def phase_lists():
    kv_local = [(r, c) for r in range(2) for c in range(2)]
    local = kv_local + [(r, c) for r in range(4) for c in range(4) if (r, c) not in kv_local]
    kv_halo = [(a, b) for a in range(-1, 2) for b in range(-1, 2) if min(a, b) < 0]
    grid = [(r, c) for r in range(-1, 4) for c in range(-1, 4) if min(r, c) < 0]
    halo = kv_halo + [p for p in grid if p not in kv_halo]
    return local, halo, len(kv_local), len(kv_halo)


def select_rows(phases, rows, cols, total, left_at, up_at, corner_at):
    kr, kc = rows // 4, cols // 4
    t = lax.broadcasted_iota(jnp.int32, (kr * kc, 1), 0)
    m = t // kc
    n = t - m * kc
    lanes = lax.broadcasted_iota(jnp.int32, (kr * kc, total), 1)
    parts = []
    for r_off, c_off in phases:
        r, c = 4 * m + r_off, 4 * n + c_off
        src = r * cols + c
        if c_off < 0:
            src = jnp.where(c < 0, left_at + r, src)
        if r_off < 0:
            src = jnp.where(r < 0, jnp.where(c < 0, corner_at, up_at + c), src)
        parts.append(jnp.where(lanes == src, 1.0, 0.0).astype(jnp.bfloat16))
    return jnp.concatenate(parts, axis=0)


def dot32(a, b):
    return jnp.dot(a, b, preferred_element_type=jnp.float32)


def section_kernel(
    nr, nc, patches, gain, w_hbm, pool_q, pool_kv, out,
    ext, col_out, col_in, row_in, cor_in, kv_out, kv_all, q_out, q_in, att_out, att_in,
    w_qkv, v_turned, acc, peak, summed,
    w_sem, h_send, h_recv, a_send, a_recv, g_send, g_recv, q_send, q_recv, o_send, o_recv,
):
    rows, cols, width = patches.shape
    head = width // HEADS
    group = width // nc
    heads = HEADS // nc
    per = (rows // 4) * (cols // 4)
    r, c = lax.axis_index("row"), lax.axis_index("col")
    side, z = lax.rem(r, 2), r // 2
    core, chip = lax.rem(c, 2), c // 2
    partner = r + 1 - 2 * side
    steps, pairs = nr // 2, nc // 2
    local = rows * cols
    left_at, up_at = local, local + rows
    corner_at = up_at + cols + cols - 1
    total = ext.shape[0]

    w_copies = [
        pltpu.make_async_copy(
            w_hbm.at[:, i * width : (i + 1) * width],
            w_qkv.at[:, i * width : (i + 1) * width],
            w_sem.at[i],
        )
        for i in range(3)
    ]
    for copy in w_copies:
        copy.start()

    def peer(j):
        return 2 * lax.rem(chip + 1 + j // 2, pairs) + lax.rem(core + 1 + j, 2)

    peers = [peer(j) for j in range(nc - 1)]
    barrier = pltpu.get_barrier_semaphore()

    def greet(to):
        pl.semaphore_signal(barrier, inc=1, device_id=to, device_id_type=MESH)

    for to in peers:
        greet((r, to))
    pl.when(r > 0)(lambda: greet((r - 1, c)))
    pl.when(r < nr - 1)(lambda: greet((r + 1, c)))
    pl.when((r > 0) & (c > 0))(lambda: greet((r - 1, c - 1)))
    pl.when((r < nr - 1) & (c < nc - 1))(lambda: greet((r + 1, c + 1)))
    pl.when(r > 1)(lambda: greet((r - 2, c)))
    pl.when(r < nr - 2)(lambda: greet((r + 2, c)))

    for i in range(rows // 8):
        col_out[8 * i : 8 * i + 8] = patches[8 * i : 8 * i + 8, cols - 1, :]

    weight = gain[...].reshape(1, width)

    def norm(block):
        values = block.astype(jnp.float32)
        center = values - jnp.mean(values, axis=-1, keepdims=True)
        spread = jnp.mean(center * center, axis=-1, keepdims=True)
        return (center * lax.rsqrt(spread + 1e-06) * weight).astype(jnp.bfloat16)

    piece = 4

    def norm_step(i, carry):
        block = patches[pl.ds(i * piece, piece)].reshape(piece * cols, width)
        at = pl.multiple_of(i * piece * cols, piece * cols)
        ext[pl.ds(at, piece * cols), :] = norm(block)
        return carry

    early = rows // piece // 2
    lax.fori_loop(0, early, norm_step, 0, unroll=True)

    def one_if(yes):
        return jnp.where(yes, 1, 0)

    greeters = nc - 1 + one_if(r > 0) + one_if(r < nr - 1) + one_if(r > 1) + one_if(r < nr - 2)
    greeters += one_if((r > 0) & (c > 0)) + one_if((r < nr - 1) & (c < nc - 1))
    pl.semaphore_wait(barrier, greeters)

    def remote(src, dst, send, recv, to):
        return pltpu.make_async_remote_copy(
            src_ref=src, dst_ref=dst, send_sem=send, recv_sem=recv,
            device_id=to, device_id_type=MESH,
        )

    row_copy = remote(patches.at[rows - 1], row_in, h_send.at[0], h_recv.at[0], (r + 1, c))
    col_copy = remote(col_out, col_in, h_send.at[1], h_recv.at[1], (r, c + 1))
    cor_copy = remote(patches.at[rows - 1], cor_in, h_send.at[2], h_recv.at[2], (r + 1, c + 1))
    pl.when((r < nr - 1) & (c < nc - 1))(lambda: cor_copy.start())
    pl.when(r < nr - 1)(lambda: row_copy.start())
    pl.when(c < nc - 1)(lambda: col_copy.start())

    lax.fori_loop(early, rows // piece, norm_step, 0, unroll=True)

    local_phases, halo_phases, n_kv_local, n_kv_halo = phase_lists()
    place = (rows, cols)
    marks = (left_at, up_at, corner_at)
    x_local = dot32(select_rows(local_phases, *place, local, *marks), ext[0:local, :])
    x_local = x_local.astype(jnp.bfloat16)

    def project(x, part):
        lanes = slice(part * width, (part + 1) * width)
        return dot32(x, w_qkv[:, lanes]).astype(jnp.bfloat16)

    w_copies[0].wait()
    q_proj = {0: project(x_local, 0)}
    w_copies[1].wait()
    w_copies[2].wait()
    kv_proj = {(0, half): project(x_local[: n_kv_local * per], 1 + half) for half in range(2)}

    def halo(present, copy, source, at, count):
        @pl.when(present)
        def _():
            copy.wait_recv()
            ext[at : at + count, :] = norm(source[...])

        @pl.when(jnp.logical_not(present))
        def _():
            ext[at : at + count, :] = jnp.zeros((count, width), jnp.bfloat16)

    halo(r > 0, row_copy, row_in, up_at, cols)
    halo(c > 0, col_copy, col_in, left_at, rows)
    halo((r > 0) & (c > 0), cor_copy, cor_in, up_at + cols, cols)

    x_halo = dot32(select_rows(halo_phases, *place, total, *marks), ext[...])
    x_halo = x_halo.astype(jnp.bfloat16)
    for half in range(2):
        kv_proj[1, half] = project(x_halo[: n_kv_halo * per], 1 + half)

    found = {p: (0, i) for i, p in enumerate(local_phases)}
    found.update({p: (1, i) for i, p in enumerate(halo_phases)})

    def pooled(values, taps, lanes, base_r, base_c):
        total_term = None
        for a in range(3):
            for b in range(3):
                which, k = found[base_r + a - 1, base_c + b - 1]
                tap = taps[3 * a + b : 3 * a + b + 1, lanes]
                term = tap * values[which][k * per : (k + 1) * per].astype(jnp.float32)
                total_term = term if total_term is None else total_term + term
        return total_term.astype(jnp.bfloat16)

    for half in range(2):
        lanes = slice(half * width, (half + 1) * width)
        got = pooled({w: kv_proj[w, half] for w in range(2)}, pool_kv, lanes, 0, 0)
        for g in range(nc):
            kv_out[g, :, half * group : (half + 1) * group] = got[:, g * group : (g + 1) * group]

    def kv_copy(j, to):
        mine = kv_all.at[side, z, chip, core]
        return remote(kv_out.at[to], mine, a_send.at[j], a_recv.at[c], (r, to))

    def kv_wait(j, to):
        slot = kv_all.at[side, z, to // 2, lax.rem(to, 2)]
        remote(kv_out.at[to], slot, a_send.at[j], a_recv.at[to], (r, to)).wait_recv()

    kv_copies = [kv_copy(j, to) for j, to in enumerate(peers)]
    for copy in kv_copies:
        copy.start()
    kv_all[side, z, chip, core] = kv_out[c]

    def relay(level, pair, lane, to):
        slot = kv_all.at[side, level, pair]
        return remote(slot, slot, g_send.at[lane, level, pair], g_recv.at[side, level, pair], to)

    def send_along(level, pair, lane, start):
        to_row = (r + 2, r - 2, partner)[lane]
        copy = relay(level, pair, lane, (to_row, c))

        def act():
            copy.start() if start else copy.wait_send()

        if lane == 0:
            pl.when(z + 1 < steps)(act)
        elif lane == 1:
            pl.when(z >= 1)(act)
        else:
            act()

    def chunk(j):
        return lax.rem(chip + j, pairs)

    def own(j, start):
        for lane in range(3):
            send_along(z, chunk(j), lane, start)

    def each(step, j, start):
        for level, there, lane in ((z - step, z - step >= 0, 0), (z + step, z + step < steps, 1)):

            @pl.when(there)
            def _():
                if start:
                    relay(level, chunk(j), lane, (partner, c)).wait_recv()
                send_along(level, chunk(j), lane, start)
                send_along(level, chunk(j), 2, start)

    q_proj[1] = project(x_halo, 0)
    kv_wait(nc - 2, peers[nc - 2])
    own(0, True)

    parts = [
        pooled(q_proj, pool_q, slice(0, width), 2 * p, 2 * q) for p in range(2) for q in range(2)
    ]
    mixed_order = jnp.concatenate(parts, axis=0)
    count = 4 * per
    t = lax.broadcasted_iota(jnp.int32, (count, 1), 0)
    q_row = t // (cols // 2)
    q_col = t - q_row * (cols // 2)
    which = 2 * lax.rem(q_row, 2) + lax.rem(q_col, 2)
    src = which * per + (q_row // 2) * (cols // 4) + q_col // 2
    lanes = lax.broadcasted_iota(jnp.int32, (count, count), 1)
    order = jnp.where(lanes == src, 1.0, 0.0).astype(jnp.bfloat16)
    natural = dot32(order, mixed_order).astype(jnp.bfloat16)
    wide = q_out.shape[2]
    for g in range(nc):
        piece_q = natural[:, g * group : (g + 1) * group]
        q_out[g] = jnp.concatenate(
            [piece_q, jnp.zeros((count, wide - group), jnp.bfloat16)], axis=1
        )

    def q_copy(j, to):
        return remote(q_out.at[to], q_in.at[c], q_send.at[j], q_recv.at[c], (r, to))

    q_copies = [q_copy(j, to) for j, to in enumerate(peers)]
    for copy in q_copies:
        copy.start()
    q_in[c] = q_out[c]

    for j in range(nc - 2):
        kv_wait(j, peers[j])
    for j in range(1, pairs):
        own(j, True)
    for step in range(1, steps):
        for j in range(pairs):
            each(step, j, True)
    for j, to in enumerate(peers):
        remote(q_out.at[to], q_in.at[to], q_send.at[j], q_recv.at[to], (r, to)).wait_recv()

    keys = steps * nc * per
    factor = float(head) ** (-0.5) * math.log2(math.e)
    kv_lanes = 2 * group
    lane = lax.broadcasted_iota(jnp.int32, (count, wide), 1)
    shift = wide - group

    def scores_of(g, from_side):
        q = q_in[g]
        stacked = jnp.concatenate(
            [
                jnp.where((lane >= h * head) & (lane < (h + 1) * head), q, jnp.zeros_like(q))
                for h in range(heads)
            ],
            axis=0,
        )
        k_part = kv_all[from_side, :, :, :, :, 0:wide].reshape(keys, wide)
        return lax.dot_general(
            k_part, stacked, (((1,), (1,)), ((), ())), preferred_element_type=jnp.float32
        )

    def turn_values(from_side):
        v_part = kv_all[from_side, :, :, :, :, kv_lanes - wide : kv_lanes].reshape(keys, wide)
        v_turned[...] = v_part.T[shift:, :]

    def weighted(expo):
        return dot32(v_turned[...], expo.astype(jnp.bfloat16))

    turn_values(side)

    def first_half(g, carry):
        scores = scores_of(g, side)
        top = jnp.max(scores, axis=0, keepdims=True)
        expo = jnp.exp2((scores - top) * factor)
        peak[g] = top
        summed[g] = jnp.sum(expo, axis=0, keepdims=True)
        acc[g] = weighted(expo)
        return carry

    lax.fori_loop(0, nc, first_half, 0)

    for level in range(steps):
        for pair in range(pairs):
            slot = kv_all.at[1 - side, level, pair]
            remote(
                slot, slot, g_send.at[2, level, pair], g_recv.at[1 - side, level, pair],
                (partner, c),
            ).wait_recv()

    def second_half(g):
        scores = scores_of(g, 1 - side)
        before = peak[g]
        top = jnp.maximum(before, jnp.max(scores, axis=0, keepdims=True))
        expo = jnp.exp2((scores - top) * factor)
        fade = jnp.exp2((before - top) * factor)
        whole = summed[g] * fade + jnp.sum(expo, axis=0, keepdims=True)
        numer = (acc[g] * fade + weighted(expo)) / whole
        picked = [
            numer[h * head : (h + 1) * head, h * count : (h + 1) * count] for h in range(heads)
        ]
        att_out[g] = jnp.concatenate(picked, axis=0).astype(jnp.bfloat16)

    turn_values(1 - side)

    def att_copy(j, to):
        return remote(att_out.at[to], att_in.at[c], o_send.at[j], o_recv.at[c], (r, to))

    def second_step(j, carry):
        to = peer(j)
        second_half(to)
        att_copy(j, to).start()
        return carry

    lax.fori_loop(0, nc - 1, second_step, 0)
    second_half(c)
    att_in[c] = att_out[c]
    for j, to in enumerate(peers):
        remote(att_out.at[to], att_in.at[to], o_send.at[j], o_recv.at[to], (r, to)).wait_recv()
    for g in range(nc):
        out[g * group : (g + 1) * group, :] = att_in[g]

    pl.when(r < nr - 1)(lambda: row_copy.wait_send())
    pl.when(c < nc - 1)(lambda: col_copy.wait_send())
    pl.when((r < nr - 1) & (c < nc - 1))(lambda: cor_copy.wait_send())
    for copy in kv_copies + q_copies:
        copy.wait_send()
    for j, to in enumerate(peers):
        att_copy(j, to).wait_send()
    for j in range(pairs):
        own(j, False)
    for step in range(1, steps):
        for j in range(pairs):
            each(step, j, False)


def by_kernel(nr, nc, patches, norm_gain, w_qkv, pool_q, pool_kv, w_out):
    rows, cols, width = patches.shape
    per = (rows // 4) * (cols // 4)
    count = 4 * per
    group = width // nc
    heads = HEADS // nc
    wide = -(-group // 128) * 128
    total = rows * cols + rows + 2 * cols
    total = -(-total // 16) * 16
    steps, pairs = nr // 2, nc // 2
    bf16, f32 = jnp.bfloat16, jnp.float32
    dma = pltpu.SemaphoreType.DMA
    vmem = pl.BlockSpec(memory_space=pltpu.VMEM)
    attended = pl.pallas_call(
        functools.partial(section_kernel, nr, nc),
        out_shape=jax.ShapeDtypeStruct((width, count), bf16),
        in_specs=[vmem, vmem, pl.BlockSpec(memory_space=pl.ANY), vmem, vmem],
        out_specs=vmem,
        scratch_shapes=[
            pltpu.VMEM((total, width), bf16),
            pltpu.VMEM((rows, width), bf16),
            pltpu.VMEM((rows, width), bf16),
            pltpu.VMEM((cols, width), bf16),
            pltpu.VMEM((cols, width), bf16),
            pltpu.VMEM((nc, per, 2 * group), bf16),
            pltpu.VMEM((2, steps, pairs, 2, per, 2 * group), bf16),
            pltpu.VMEM((nc, count, wide), bf16),
            pltpu.VMEM((nc, count, wide), bf16),
            pltpu.VMEM((nc, group, count), bf16),
            pltpu.VMEM((nc, group, count), bf16),
            pltpu.VMEM(w_qkv.shape, bf16),
            pltpu.VMEM((group, steps * nc * per), bf16),
            pltpu.VMEM((nc, group, heads * count), f32),
            pltpu.VMEM((nc, 1, heads * count), f32),
            pltpu.VMEM((nc, 1, heads * count), f32),
            dma((3,)),
            dma((3,)), dma((3,)),
            dma((nc,)), dma((nc,)),
            dma((3, steps, pairs)), dma((2, steps, pairs)),
            dma((nc,)), dma((nc,)),
            dma((nc,)), dma((nc,)),
        ],
        compiler_params=pltpu.CompilerParams(
            collective_id=0, has_side_effects=True, vmem_limit_bytes=56 * 1024 * 1024
        ),
    )(patches, norm_gain, w_qkv, pool_q, pool_kv)
    mixed = lax.dot_general(
        attended, w_out, (((0,), (0,)), ((), ())), preferred_element_type=f32
    ).astype(bf16)
    return mixed.reshape(rows // 2, cols // 2, width)


def solution(mesh):
    nr, nc = mesh.shape["row"], mesh.shape["col"]
    placed = (P("row", "col", None), P(), P(), P(), P(), P())
    fits = nr % 2 == 0 and nc % 2 == 0 and HEADS % nc == 0
    body = functools.partial(by_kernel, nr, nc) if fits else on_device
    return jax.shard_map(
        body, mesh=mesh, in_specs=placed, out_specs=P("row", "col", None), check_vma=False
    )
```

```python
import functools
import math

import jax
import jax.numpy as jnp
from jax import lax
from jax.experimental import pallas as pl
from jax.experimental.pallas import tpu as pltpu
from jax.sharding import PartitionSpec as P

HEADS = 12
MESH = pl.DeviceIdType.MESH


def passed_along(block, axis, distance):
    devices = range(lax.axis_size(axis))
    route = [(i - distance, i) for i in devices if i - distance in devices]
    return lax.ppermute(block, axis, route)


def layer_norm(patches, norm_gain):
    values = patches.astype(jnp.float32)
    center = values - jnp.mean(values, axis=-1, keepdims=True)
    spread = jnp.mean(center * center, axis=-1, keepdims=True)
    return (center * lax.rsqrt(spread + 1e-06) * norm_gain).astype(jnp.bfloat16)


def pool_grid(padded, kernel, stride, out_rows, out_cols):
    summed = jnp.zeros((out_rows, out_cols, padded.shape[-1]), jnp.float32)
    for row_off in range(3):
        for col_off in range(3):
            window = padded[
                row_off : row_off + stride * out_rows : stride,
                col_off : col_off + stride * out_cols : stride,
            ]
            summed = summed + kernel[3 * row_off + col_off] * window.astype(jnp.float32)
    return summed.astype(jnp.bfloat16)


def make_step(queries, width):
    head_size = width // HEADS
    scale = float(head_size) ** (-0.5)

    def one_block(carry, block):
        run_max, run_sum, accum = carry
        count = block.shape[0]
        key_heads = block[:, :width].reshape(count, HEADS, head_size)
        val_heads = block[:, width:].reshape(count, HEADS, head_size)
        scores = (
            jnp.einsum("qhd,khd->hqk", queries, key_heads, preferred_element_type=jnp.float32)
            * scale
        )
        new_max = jnp.maximum(run_max, jnp.max(scores, axis=-1))
        factor = jnp.exp(run_max - new_max)
        expo = jnp.exp(scores - new_max[..., None])
        run_sum = run_sum * factor + jnp.sum(expo, axis=-1)
        weights = expo.astype(jnp.bfloat16)
        accum = accum * factor[..., None] + jnp.einsum(
            "hqk,khd->hqd", weights, val_heads, preferred_element_type=jnp.float32
        )
        return ((new_max, run_sum, accum), None)

    return one_block


def start_state(query_count, width):
    return (
        jnp.full((HEADS, query_count), -1e30, jnp.float32),
        jnp.zeros((HEADS, query_count), jnp.float32),
        jnp.zeros((HEADS, query_count, width // HEADS), jnp.float32),
    )


def fold_keys(carry, queries, keyvals, width):
    count = keyvals.shape[0]
    block_len = 512
    stacked = keyvals.reshape(count // block_len, block_len, keyvals.shape[1])
    carry, unused = lax.scan(make_step(queries, width), carry, stacked)
    return carry


def on_device(patches, norm_gain, w_qkv, pool_q, pool_kv, w_out):
    tile_rows, tile_cols, width = patches.shape
    head_size = width // HEADS
    normed = layer_norm(patches, norm_gain)
    projected = jnp.dot(normed.reshape(-1, width), w_qkv, preferred_element_type=jnp.float32)
    projected = projected.astype(jnp.bfloat16).reshape(tile_rows, tile_cols, 3 * width)
    upper = passed_along(projected[-1:], "row", 1)
    taller = jnp.concatenate([upper, projected], axis=0)
    left_rim = passed_along(taller[:, -1:], "col", 1)
    extended = jnp.concatenate([left_rim, taller], axis=1)
    query_flat = pool_grid(extended[..., :width], pool_q, 2, tile_rows // 2, tile_cols // 2)
    query_flat = query_flat.reshape(-1, width)
    keyvals = pool_grid(extended[..., width:], pool_kv, 4, tile_rows // 4, tile_cols // 4)
    keyvals = keyvals.reshape(-1, 2 * width)
    query_count = query_flat.shape[0]
    queries = query_flat.reshape(query_count, HEADS, head_size)
    every_key = lax.all_gather(keyvals, ("row", "col"), axis=0, tiled=True)
    carry = fold_keys(start_state(query_count, width), queries, every_key, width)
    run_max, run_sum, accum = carry
    attended = (
        (accum / run_sum[..., None])
        .transpose(1, 0, 2)
        .reshape(query_count, width)
        .astype(jnp.bfloat16)
    )
    mixed = jnp.dot(attended, w_out, preferred_element_type=jnp.float32).astype(jnp.bfloat16)
    return mixed.reshape(tile_rows // 2, tile_cols // 2, width)


def phase_lists():
    kv_local = [(r, c) for r in range(2) for c in range(2)]
    local = kv_local + [(r, c) for r in range(4) for c in range(4) if (r, c) not in kv_local]
    kv_halo = [(a, b) for a in range(-1, 2) for b in range(-1, 2) if min(a, b) < 0]
    grid = [(r, c) for r in range(-1, 4) for c in range(-1, 4) if min(r, c) < 0]
    halo = kv_halo + [p for p in grid if p not in kv_halo]
    return local, halo, len(kv_local), len(kv_halo)


def select_rows(phases, rows, cols, total, left_at, up_at, corner_at):
    kr, kc = rows // 4, cols // 4
    t = lax.broadcasted_iota(jnp.int32, (kr * kc, 1), 0)
    m = t // kc
    n = t - m * kc
    lanes = lax.broadcasted_iota(jnp.int32, (kr * kc, total), 1)
    parts = []
    for r_off, c_off in phases:
        r, c = 4 * m + r_off, 4 * n + c_off
        src = r * cols + c
        if c_off < 0:
            src = jnp.where(c < 0, left_at + r, src)
        if r_off < 0:
            src = jnp.where(r < 0, jnp.where(c < 0, corner_at, up_at + c), src)
        parts.append(jnp.where(lanes == src, 1.0, 0.0).astype(jnp.bfloat16))
    return jnp.concatenate(parts, axis=0)


def dot32(a, b):
    return jnp.dot(a, b, preferred_element_type=jnp.float32)


def section_kernel(
    nr, nc, patches, gain, w_hbm, pool_q, pool_kv, out,
    ext, col_out, col_in, row_in, cor_in, kv_out, kv_all, q_out, q_in, att_out, att_in,
    w_qkv, q_all, acc, peak, summed,
    w_sem, h_send, h_recv, a_send, a_recv, g_send, g_recv, q_send, q_recv, o_send, o_recv,
):
    rows, cols, width = patches.shape
    head = width // HEADS
    group = width // nc
    heads = HEADS // nc
    per = (rows // 4) * (cols // 4)
    r, c = lax.axis_index("row"), lax.axis_index("col")
    side, z = lax.rem(r, 2), r // 2
    core, chip = lax.rem(c, 2), c // 2
    partner = r + 1 - 2 * side
    steps, pairs = nr // 2, nc // 2
    local = rows * cols
    left_at, up_at = local, local + rows
    corner_at = up_at + cols + cols - 1
    total = ext.shape[0]

    w_copies = [
        pltpu.make_async_copy(
            w_hbm.at[:, i * width : (i + 1) * width],
            w_qkv.at[:, i * width : (i + 1) * width],
            w_sem.at[i],
        )
        for i in range(3)
    ]
    for copy in w_copies:
        copy.start()

    def peer(j):
        return 2 * lax.rem(chip + 1 + j // 2, pairs) + lax.rem(core + 1 + j, 2)

    peers = [peer(j) for j in range(nc - 1)]
    barrier = pltpu.get_barrier_semaphore()

    def greet(to):
        pl.semaphore_signal(barrier, inc=1, device_id=to, device_id_type=MESH)

    for to in peers:
        greet((r, to))
    pl.when(r > 0)(lambda: greet((r - 1, c)))
    pl.when(r < nr - 1)(lambda: greet((r + 1, c)))
    pl.when((r > 0) & (c > 0))(lambda: greet((r - 1, c - 1)))
    pl.when((r < nr - 1) & (c < nc - 1))(lambda: greet((r + 1, c + 1)))
    pl.when(r > 1)(lambda: greet((r - 2, c)))
    pl.when(r < nr - 2)(lambda: greet((r + 2, c)))

    for i in range(rows // 8):
        col_out[8 * i : 8 * i + 8] = patches[8 * i : 8 * i + 8, cols - 1, :]

    weight = gain[...].reshape(1, width)

    def norm(block):
        values = block.astype(jnp.float32)
        center = values - jnp.mean(values, axis=-1, keepdims=True)
        spread = jnp.mean(center * center, axis=-1, keepdims=True)
        return (center * lax.rsqrt(spread + 1e-06) * weight).astype(jnp.bfloat16)

    piece = 4

    def norm_step(i, carry):
        block = patches[pl.ds(i * piece, piece)].reshape(piece * cols, width)
        at = pl.multiple_of(i * piece * cols, piece * cols)
        ext[pl.ds(at, piece * cols), :] = norm(block)
        return carry

    early = rows // piece // 2
    lax.fori_loop(0, early, norm_step, 0, unroll=True)

    def one_if(yes):
        return jnp.where(yes, 1, 0)

    greeters = nc - 1 + one_if(r > 0) + one_if(r < nr - 1) + one_if(r > 1) + one_if(r < nr - 2)
    greeters += one_if((r > 0) & (c > 0)) + one_if((r < nr - 1) & (c < nc - 1))
    pl.semaphore_wait(barrier, greeters)

    def remote(src, dst, send, recv, to):
        return pltpu.make_async_remote_copy(
            src_ref=src, dst_ref=dst, send_sem=send, recv_sem=recv,
            device_id=to, device_id_type=MESH,
        )

    row_copy = remote(patches.at[rows - 1], row_in, h_send.at[0], h_recv.at[0], (r + 1, c))
    col_copy = remote(col_out, col_in, h_send.at[1], h_recv.at[1], (r, c + 1))
    cor_copy = remote(patches.at[rows - 1], cor_in, h_send.at[2], h_recv.at[2], (r + 1, c + 1))
    pl.when((r < nr - 1) & (c < nc - 1))(lambda: cor_copy.start())
    pl.when(r < nr - 1)(lambda: row_copy.start())
    pl.when(c < nc - 1)(lambda: col_copy.start())

    lax.fori_loop(early, rows // piece, norm_step, 0, unroll=True)

    local_phases, halo_phases, n_kv_local, n_kv_halo = phase_lists()
    place = (rows, cols)
    marks = (left_at, up_at, corner_at)
    x_local = dot32(select_rows(local_phases, *place, local, *marks), ext[0:local, :])
    x_local = x_local.astype(jnp.bfloat16)

    def project(x, part):
        lanes = slice(part * width, (part + 1) * width)
        return dot32(x, w_qkv[:, lanes]).astype(jnp.bfloat16)

    w_copies[0].wait()
    q_proj = {0: project(x_local, 0)}
    w_copies[1].wait()
    w_copies[2].wait()
    kv_proj = {(0, half): project(x_local[: n_kv_local * per], 1 + half) for half in range(2)}

    def halo(present, copy, source, at, count):
        @pl.when(present)
        def _():
            copy.wait_recv()
            ext[at : at + count, :] = norm(source[...])

        @pl.when(jnp.logical_not(present))
        def _():
            ext[at : at + count, :] = jnp.zeros((count, width), jnp.bfloat16)

    halo(r > 0, row_copy, row_in, up_at, cols)
    halo(c > 0, col_copy, col_in, left_at, rows)
    halo((r > 0) & (c > 0), cor_copy, cor_in, up_at + cols, cols)

    x_halo = dot32(select_rows(halo_phases, *place, total, *marks), ext[...])
    x_halo = x_halo.astype(jnp.bfloat16)
    for half in range(2):
        kv_proj[1, half] = project(x_halo[: n_kv_halo * per], 1 + half)

    found = {p: (0, i) for i, p in enumerate(local_phases)}
    found.update({p: (1, i) for i, p in enumerate(halo_phases)})

    def pooled(values, taps, lanes, base_r, base_c):
        total_term = None
        for a in range(3):
            for b in range(3):
                which, k = found[base_r + a - 1, base_c + b - 1]
                tap = taps[3 * a + b : 3 * a + b + 1, lanes]
                term = tap * values[which][k * per : (k + 1) * per].astype(jnp.float32)
                total_term = term if total_term is None else total_term + term
        return total_term.astype(jnp.bfloat16)

    for half in range(2):
        lanes = slice(half * width, (half + 1) * width)
        got = pooled({w: kv_proj[w, half] for w in range(2)}, pool_kv, lanes, 0, 0)
        for g in range(nc):
            kv_out[g, :, half * group : (half + 1) * group] = got[:, g * group : (g + 1) * group]

    def kv_copy(j, to):
        mine = kv_all.at[side, z, chip, core]
        return remote(kv_out.at[to], mine, a_send.at[j], a_recv.at[c], (r, to))

    def kv_wait(j, to):
        slot = kv_all.at[side, z, to // 2, lax.rem(to, 2)]
        remote(kv_out.at[to], slot, a_send.at[j], a_recv.at[to], (r, to)).wait_recv()

    kv_copies = [kv_copy(j, to) for j, to in enumerate(peers)]
    for copy in kv_copies:
        copy.start()
    kv_all[side, z, chip, core] = kv_out[c]

    def relay(level, pair, lane, to):
        slot = kv_all.at[side, level, pair]
        return remote(slot, slot, g_send.at[lane, level, pair], g_recv.at[side, level, pair], to)

    def send_along(level, pair, lane, start):
        to_row = (r + 2, r - 2, partner)[lane]
        copy = relay(level, pair, lane, (to_row, c))

        def act():
            copy.start() if start else copy.wait_send()

        if lane == 0:
            pl.when(z + 1 < steps)(act)
        elif lane == 1:
            pl.when(z >= 1)(act)
        else:
            act()

    def chunk(j):
        return lax.rem(chip + j, pairs)

    def own(j, start):
        for lane in range(3):
            send_along(z, chunk(j), lane, start)

    def each(step, j, start):
        for level, there, lane in ((z - step, z - step >= 0, 0), (z + step, z + step < steps, 1)):

            @pl.when(there)
            def _():
                if start:
                    relay(level, chunk(j), lane, (partner, c)).wait_recv()
                send_along(level, chunk(j), lane, start)
                send_along(level, chunk(j), 2, start)

    q_proj[1] = project(x_halo, 0)
    kv_wait(nc - 2, peers[nc - 2])
    own(0, True)

    parts = [
        pooled(q_proj, pool_q, slice(0, width), 2 * p, 2 * q) for p in range(2) for q in range(2)
    ]
    mixed_order = jnp.concatenate(parts, axis=0)
    count = 4 * per
    t = lax.broadcasted_iota(jnp.int32, (count, 1), 0)
    q_row = t // (cols // 2)
    q_col = t - q_row * (cols // 2)
    which = 2 * lax.rem(q_row, 2) + lax.rem(q_col, 2)
    src = which * per + (q_row // 2) * (cols // 4) + q_col // 2
    lanes = lax.broadcasted_iota(jnp.int32, (count, count), 1)
    order = jnp.where(lanes == src, 1.0, 0.0).astype(jnp.bfloat16)
    natural = dot32(order, mixed_order).astype(jnp.bfloat16)
    wide = q_out.shape[2]
    for g in range(nc):
        piece_q = natural[:, g * group : (g + 1) * group]
        q_out[g] = jnp.concatenate(
            [piece_q, jnp.zeros((count, wide - group), jnp.bfloat16)], axis=1
        )

    def q_copy(j, to):
        return remote(q_out.at[to], q_in.at[c], q_send.at[j], q_recv.at[c], (r, to))

    q_copies = [q_copy(j, to) for j, to in enumerate(peers)]
    for copy in q_copies:
        copy.start()
    q_in[c] = q_out[c]

    for j in range(nc - 2):
        kv_wait(j, peers[j])
    for j in range(1, pairs):
        own(j, True)
    keys = nc * per
    factor = float(head) ** (-0.5) * math.log2(math.e)
    kv_lanes = 2 * group
    lane = lax.broadcasted_iota(jnp.int32, (count, wide), 1)
    shift = wide - group
    stack = heads * count

    def stack_queries():
        for j, to in enumerate(peers):
            remote(q_out.at[to], q_in.at[to], q_send.at[j], q_recv.at[to], (r, to)).wait_recv()
        for g in range(nc):
            q = q_in[g]
            for h in range(heads):
                kept = (lane >= h * head) & (lane < (h + 1) * head)
                at = g * stack + h * count
                q_all[at : at + count, :] = jnp.where(kept, q, jnp.zeros_like(q))

    def absorb(from_side, level, first=False):
        k_part = kv_all[from_side, level, :, :, :, 0:wide].reshape(keys, wide)
        v_part = kv_all[from_side, level, :, :, :, kv_lanes - wide : kv_lanes].reshape(keys, wide)
        scores = lax.dot_general(
            k_part, q_all[...], (((1,), (1,)), ((), ())), preferred_element_type=jnp.float32
        )
        high = jnp.max(scores, axis=0, keepdims=True)
        top = high if first else jnp.maximum(peak[...], high)
        expo = jnp.exp2((scores - top) * factor)
        piece_sum = jnp.sum(expo, axis=0, keepdims=True)
        numer = dot32(v_part.T[shift:, :], expo.astype(jnp.bfloat16))
        if first:
            summed[...] = piece_sum
            acc[...] = numer
        else:
            fade = jnp.exp2((peak[...] - top) * factor)
            summed[...] = summed[...] * fade + piece_sum
            acc[...] = acc[...] * fade + numer
        peak[...] = top

    def absorb_both(step, visit):
        def one(k, carry):
            level = z - step + 2 * k * step
            pl.when((level >= 0) & (level < steps))(lambda: visit(level))
            return carry

        lax.fori_loop(0, 2, one, 0)

    for j in range(pairs):
        each(1, j, True)
    stack_queries()
    absorb(side, z, True)

    def own_step(step, carry):
        absorb_both(step, lambda level: absorb(side, level))
        for j in range(pairs):
            each(step + 1, j, True)
        return carry

    lax.fori_loop(1, steps, own_step, 0)

    def from_partner(level):
        for pair in range(pairs):
            slot = kv_all.at[1 - side, level, pair]
            remote(
                slot, slot, g_send.at[2, level, pair], g_recv.at[1 - side, level, pair],
                (partner, c),
            ).wait_recv()
        absorb(1 - side, level)

    def partner_step(k, carry):
        step = (k + 1) // 2
        level = z + step * (2 * lax.rem(k, 2) - 1)
        pl.when((level >= 0) & (level < steps))(lambda: from_partner(level))
        return carry

    lax.fori_loop(0, 2 * steps - 1, partner_step, 0)

    def finish(g):
        lanes_g = pl.ds(pl.multiple_of(g * stack, 128), stack)
        numer = acc[:, lanes_g] / summed[:, lanes_g]
        picked = [
            numer[h * head : (h + 1) * head, h * count : (h + 1) * count] for h in range(heads)
        ]
        att_out[g] = jnp.concatenate(picked, axis=0).astype(jnp.bfloat16)

    def att_copy(j, to):
        return remote(att_out.at[to], att_in.at[c], o_send.at[j], o_recv.at[c], (r, to))

    def second_step(j, carry):
        to = peer(j)
        finish(to)
        att_copy(j, to).start()
        return carry

    lax.fori_loop(0, nc - 1, second_step, 0)
    finish(c)
    att_in[c] = att_out[c]
    for j, to in enumerate(peers):
        remote(att_out.at[to], att_in.at[to], o_send.at[j], o_recv.at[to], (r, to)).wait_recv()
    for g in range(nc):
        out[g * group : (g + 1) * group, :] = att_in[g]

    pl.when(r < nr - 1)(lambda: row_copy.wait_send())
    pl.when(c < nc - 1)(lambda: col_copy.wait_send())
    pl.when((r < nr - 1) & (c < nc - 1))(lambda: cor_copy.wait_send())
    for copy in kv_copies + q_copies:
        copy.wait_send()
    for j, to in enumerate(peers):
        att_copy(j, to).wait_send()
    for j in range(pairs):
        own(j, False)
    for step in range(1, steps):
        for j in range(pairs):
            each(step, j, False)


def by_kernel(nr, nc, patches, norm_gain, w_qkv, pool_q, pool_kv, w_out):
    rows, cols, width = patches.shape
    per = (rows // 4) * (cols // 4)
    count = 4 * per
    group = width // nc
    heads = HEADS // nc
    wide = -(-group // 128) * 128
    total = rows * cols + rows + 2 * cols
    total = -(-total // 16) * 16
    steps, pairs = nr // 2, nc // 2
    bf16, f32 = jnp.bfloat16, jnp.float32
    dma = pltpu.SemaphoreType.DMA
    vmem = pl.BlockSpec(memory_space=pltpu.VMEM)
    attended = pl.pallas_call(
        functools.partial(section_kernel, nr, nc),
        out_shape=jax.ShapeDtypeStruct((width, count), bf16),
        in_specs=[vmem, vmem, pl.BlockSpec(memory_space=pl.ANY), vmem, vmem],
        out_specs=vmem,
        scratch_shapes=[
            pltpu.VMEM((total, width), bf16),
            pltpu.VMEM((rows, width), bf16),
            pltpu.VMEM((rows, width), bf16),
            pltpu.VMEM((cols, width), bf16),
            pltpu.VMEM((cols, width), bf16),
            pltpu.VMEM((nc, per, 2 * group), bf16),
            pltpu.VMEM((2, steps, pairs, 2, per, 2 * group), bf16),
            pltpu.VMEM((nc, count, wide), bf16),
            pltpu.VMEM((nc, count, wide), bf16),
            pltpu.VMEM((nc, group, count), bf16),
            pltpu.VMEM((nc, group, count), bf16),
            pltpu.VMEM(w_qkv.shape, bf16),
            pltpu.VMEM((nc * heads * count, wide), bf16),
            pltpu.VMEM((group, nc * heads * count), f32),
            pltpu.VMEM((1, nc * heads * count), f32),
            pltpu.VMEM((1, nc * heads * count), f32),
            dma((3,)),
            dma((3,)), dma((3,)),
            dma((nc,)), dma((nc,)),
            dma((3, steps, pairs)), dma((2, steps, pairs)),
            dma((nc,)), dma((nc,)),
            dma((nc,)), dma((nc,)),
        ],
        compiler_params=pltpu.CompilerParams(
            collective_id=0, has_side_effects=True, vmem_limit_bytes=56 * 1024 * 1024
        ),
    )(patches, norm_gain, w_qkv, pool_q, pool_kv)
    mixed = lax.dot_general(
        attended, w_out, (((0,), (0,)), ((), ())), preferred_element_type=f32
    ).astype(bf16)
    return mixed.reshape(rows // 2, cols // 2, width)


def solution(mesh):
    nr, nc = mesh.shape["row"], mesh.shape["col"]
    placed = (P("row", "col", None), P(), P(), P(), P(), P())
    fits = nr % 2 == 0 and nc % 2 == 0 and HEADS % nc == 0
    body = functools.partial(by_kernel, nr, nc) if fits else on_device
    return jax.shard_map(
        body, mesh=mesh, in_specs=placed, out_specs=P("row", "col", None), check_vma=False
    )
```

```python
import functools
import math

import jax
import jax.numpy as jnp
from jax import lax
from jax.experimental import pallas as pl
from jax.experimental.pallas import tpu as pltpu
from jax.sharding import PartitionSpec as P

HEADS = 12
MESH = pl.DeviceIdType.MESH


def passed_along(block, axis, distance):
    devices = range(lax.axis_size(axis))
    route = [(i - distance, i) for i in devices if i - distance in devices]
    return lax.ppermute(block, axis, route)


def layer_norm(patches, norm_gain):
    values = patches.astype(jnp.float32)
    center = values - jnp.mean(values, axis=-1, keepdims=True)
    spread = jnp.mean(center * center, axis=-1, keepdims=True)
    return (center * lax.rsqrt(spread + 1e-06) * norm_gain).astype(jnp.bfloat16)


def pool_grid(padded, kernel, stride, out_rows, out_cols):
    summed = jnp.zeros((out_rows, out_cols, padded.shape[-1]), jnp.float32)
    for row_off in range(3):
        for col_off in range(3):
            window = padded[
                row_off : row_off + stride * out_rows : stride,
                col_off : col_off + stride * out_cols : stride,
            ]
            summed = summed + kernel[3 * row_off + col_off] * window.astype(jnp.float32)
    return summed.astype(jnp.bfloat16)


def make_step(queries, width):
    head_size = width // HEADS
    scale = float(head_size) ** (-0.5)

    def one_block(carry, block):
        run_max, run_sum, accum = carry
        count = block.shape[0]
        key_heads = block[:, :width].reshape(count, HEADS, head_size)
        val_heads = block[:, width:].reshape(count, HEADS, head_size)
        scores = (
            jnp.einsum("qhd,khd->hqk", queries, key_heads, preferred_element_type=jnp.float32)
            * scale
        )
        new_max = jnp.maximum(run_max, jnp.max(scores, axis=-1))
        factor = jnp.exp(run_max - new_max)
        expo = jnp.exp(scores - new_max[..., None])
        run_sum = run_sum * factor + jnp.sum(expo, axis=-1)
        weights = expo.astype(jnp.bfloat16)
        accum = accum * factor[..., None] + jnp.einsum(
            "hqk,khd->hqd", weights, val_heads, preferred_element_type=jnp.float32
        )
        return ((new_max, run_sum, accum), None)

    return one_block


def start_state(query_count, width):
    return (
        jnp.full((HEADS, query_count), -1e30, jnp.float32),
        jnp.zeros((HEADS, query_count), jnp.float32),
        jnp.zeros((HEADS, query_count, width // HEADS), jnp.float32),
    )


def fold_keys(carry, queries, keyvals, width):
    count = keyvals.shape[0]
    block_len = 512
    stacked = keyvals.reshape(count // block_len, block_len, keyvals.shape[1])
    carry, unused = lax.scan(make_step(queries, width), carry, stacked)
    return carry


def on_device(patches, norm_gain, w_qkv, pool_q, pool_kv, w_out):
    tile_rows, tile_cols, width = patches.shape
    head_size = width // HEADS
    normed = layer_norm(patches, norm_gain)
    projected = jnp.dot(normed.reshape(-1, width), w_qkv, preferred_element_type=jnp.float32)
    projected = projected.astype(jnp.bfloat16).reshape(tile_rows, tile_cols, 3 * width)
    upper = passed_along(projected[-1:], "row", 1)
    taller = jnp.concatenate([upper, projected], axis=0)
    left_rim = passed_along(taller[:, -1:], "col", 1)
    extended = jnp.concatenate([left_rim, taller], axis=1)
    query_flat = pool_grid(extended[..., :width], pool_q, 2, tile_rows // 2, tile_cols // 2)
    query_flat = query_flat.reshape(-1, width)
    keyvals = pool_grid(extended[..., width:], pool_kv, 4, tile_rows // 4, tile_cols // 4)
    keyvals = keyvals.reshape(-1, 2 * width)
    query_count = query_flat.shape[0]
    queries = query_flat.reshape(query_count, HEADS, head_size)
    every_key = lax.all_gather(keyvals, ("row", "col"), axis=0, tiled=True)
    carry = fold_keys(start_state(query_count, width), queries, every_key, width)
    run_max, run_sum, accum = carry
    attended = (
        (accum / run_sum[..., None])
        .transpose(1, 0, 2)
        .reshape(query_count, width)
        .astype(jnp.bfloat16)
    )
    mixed = jnp.dot(attended, w_out, preferred_element_type=jnp.float32).astype(jnp.bfloat16)
    return mixed.reshape(tile_rows // 2, tile_cols // 2, width)


def phase_lists():
    kv_local = [(r, c) for r in range(2) for c in range(2)]
    local = kv_local + [(r, c) for r in range(4) for c in range(4) if (r, c) not in kv_local]
    kv_halo = [(a, b) for a in range(-1, 2) for b in range(-1, 2) if min(a, b) < 0]
    grid = [(r, c) for r in range(-1, 4) for c in range(-1, 4) if min(r, c) < 0]
    halo = kv_halo + [p for p in grid if p not in kv_halo]
    return local, halo, len(kv_local), len(kv_halo)


def select_rows(phases, rows, cols, total, left_at, up_at, corner_at):
    kr, kc = rows // 4, cols // 4
    t = lax.broadcasted_iota(jnp.int32, (kr * kc, 1), 0)
    m = t // kc
    n = t - m * kc
    lanes = lax.broadcasted_iota(jnp.int32, (kr * kc, total), 1)
    parts = []
    for r_off, c_off in phases:
        r, c = 4 * m + r_off, 4 * n + c_off
        src = r * cols + c
        if c_off < 0:
            src = jnp.where(c < 0, left_at + r, src)
        if r_off < 0:
            src = jnp.where(r < 0, jnp.where(c < 0, corner_at, up_at + c), src)
        parts.append(jnp.where(lanes == src, 1.0, 0.0).astype(jnp.bfloat16))
    return jnp.concatenate(parts, axis=0)


def dot32(a, b):
    return jnp.dot(a, b, preferred_element_type=jnp.float32)


def section_kernel(
    nr, nc, patches, gain, w_hbm, pool_q, pool_kv, out,
    ext, col_out, col_in, row_in, cor_in, kv_out, kv_all, q_out, q_in, att_out, att_in,
    w_qkv, q_all, acc, peak, summed,
    w_sem, h_send, h_recv, a_send, a_recv, g_send, g_recv, q_send, q_recv, o_send, o_recv,
):
    rows, cols, width = patches.shape
    head = width // HEADS
    group = width // nc
    heads = HEADS // nc
    per = (rows // 4) * (cols // 4)
    r, c = lax.axis_index("row"), lax.axis_index("col")
    side, z = lax.rem(r, 2), r // 2
    core, chip = lax.rem(c, 2), c // 2
    partner = r + 1 - 2 * side
    steps, pairs = nr // 2, nc // 2
    local = rows * cols
    left_at, up_at = local, local + rows
    corner_at = up_at + cols + cols - 1
    total = ext.shape[0]

    w_copies = [
        pltpu.make_async_copy(
            w_hbm.at[:, i * width : (i + 1) * width],
            w_qkv.at[:, i * width : (i + 1) * width],
            w_sem.at[i],
        )
        for i in range(3)
    ]
    for copy in w_copies:
        copy.start()

    def peer(j):
        return 2 * lax.rem(chip + 1 + j // 2, pairs) + lax.rem(core + 1 + j, 2)

    peers = [peer(j) for j in range(nc - 1)]
    barrier = pltpu.get_barrier_semaphore()

    def greet(to):
        pl.semaphore_signal(barrier, inc=1, device_id=to, device_id_type=MESH)

    for to in peers:
        greet((r, to))
    pl.when(r > 0)(lambda: greet((r - 1, c)))
    pl.when(r < nr - 1)(lambda: greet((r + 1, c)))
    pl.when((r > 0) & (c > 0))(lambda: greet((r - 1, c - 1)))
    pl.when((r < nr - 1) & (c < nc - 1))(lambda: greet((r + 1, c + 1)))
    pl.when(r > 1)(lambda: greet((r - 2, c)))
    pl.when(r < nr - 2)(lambda: greet((r + 2, c)))

    for i in range(rows // 8):
        col_out[8 * i : 8 * i + 8] = patches[8 * i : 8 * i + 8, cols - 1, :]

    weight = gain[...].reshape(1, width)

    def norm(block):
        values = block.astype(jnp.float32)
        center = values - jnp.mean(values, axis=-1, keepdims=True)
        spread = jnp.mean(center * center, axis=-1, keepdims=True)
        return (center * lax.rsqrt(spread + 1e-06) * weight).astype(jnp.bfloat16)

    piece = 4

    def norm_step(i, carry):
        block = patches[pl.ds(i * piece, piece)].reshape(piece * cols, width)
        at = pl.multiple_of(i * piece * cols, piece * cols)
        ext[pl.ds(at, piece * cols), :] = norm(block)
        return carry

    early = rows // piece // 2
    lax.fori_loop(0, early, norm_step, 0, unroll=True)

    def one_if(yes):
        return jnp.where(yes, 1, 0)

    greeters = nc - 1 + one_if(r > 0) + one_if(r < nr - 1) + one_if(r > 1) + one_if(r < nr - 2)
    greeters += one_if((r > 0) & (c > 0)) + one_if((r < nr - 1) & (c < nc - 1))
    pl.semaphore_wait(barrier, greeters)

    def remote(src, dst, send, recv, to):
        return pltpu.make_async_remote_copy(
            src_ref=src, dst_ref=dst, send_sem=send, recv_sem=recv,
            device_id=to, device_id_type=MESH,
        )

    row_copy = remote(patches.at[rows - 1], row_in, h_send.at[0], h_recv.at[0], (r + 1, c))
    col_copy = remote(col_out, col_in, h_send.at[1], h_recv.at[1], (r, c + 1))
    cor_copy = remote(patches.at[rows - 1], cor_in, h_send.at[2], h_recv.at[2], (r + 1, c + 1))
    pl.when((r < nr - 1) & (c < nc - 1))(lambda: cor_copy.start())
    pl.when(r < nr - 1)(lambda: row_copy.start())
    pl.when(c < nc - 1)(lambda: col_copy.start())

    lax.fori_loop(early, rows // piece, norm_step, 0, unroll=True)

    local_phases, halo_phases, n_kv_local, n_kv_halo = phase_lists()
    place = (rows, cols)
    marks = (left_at, up_at, corner_at)
    x_local = dot32(select_rows(local_phases, *place, local, *marks), ext[0:local, :])
    x_local = x_local.astype(jnp.bfloat16)

    def project(x, part):
        lanes = slice(part * width, (part + 1) * width)
        return dot32(x, w_qkv[:, lanes]).astype(jnp.bfloat16)

    w_copies[0].wait()
    q_proj = {0: project(x_local, 0)}
    w_copies[1].wait()
    w_copies[2].wait()
    kv_proj = {(0, half): project(x_local[: n_kv_local * per], 1 + half) for half in range(2)}

    def halo(present, copy, source, at, count):
        @pl.when(present)
        def _():
            copy.wait_recv()
            ext[at : at + count, :] = norm(source[...])

        @pl.when(jnp.logical_not(present))
        def _():
            ext[at : at + count, :] = jnp.zeros((count, width), jnp.bfloat16)

    halo(r > 0, row_copy, row_in, up_at, cols)
    halo(c > 0, col_copy, col_in, left_at, rows)
    halo((r > 0) & (c > 0), cor_copy, cor_in, up_at + cols, cols)

    x_halo = dot32(select_rows(halo_phases, *place, total, *marks), ext[...])
    x_halo = x_halo.astype(jnp.bfloat16)
    for half in range(2):
        kv_proj[1, half] = project(x_halo[: n_kv_halo * per], 1 + half)

    found = {p: (0, i) for i, p in enumerate(local_phases)}
    found.update({p: (1, i) for i, p in enumerate(halo_phases)})

    def pooled(values, taps, lanes, base_r, base_c):
        total_term = None
        for a in range(3):
            for b in range(3):
                which, k = found[base_r + a - 1, base_c + b - 1]
                tap = taps[3 * a + b : 3 * a + b + 1, lanes]
                term = tap * values[which][k * per : (k + 1) * per].astype(jnp.float32)
                total_term = term if total_term is None else total_term + term
        return total_term.astype(jnp.bfloat16)

    for half in range(2):
        lanes = slice(half * width, (half + 1) * width)
        got = pooled({w: kv_proj[w, half] for w in range(2)}, pool_kv, lanes, 0, 0)
        for g in range(nc):
            kv_out[g, :, half * group : (half + 1) * group] = got[:, g * group : (g + 1) * group]

    def kv_copy(j, to):
        mine = kv_all.at[side, z, chip, core]
        return remote(kv_out.at[to], mine, a_send.at[j], a_recv.at[c], (r, to))

    def kv_wait(j, to):
        slot = kv_all.at[side, z, to // 2, lax.rem(to, 2)]
        remote(kv_out.at[to], slot, a_send.at[j], a_recv.at[to], (r, to)).wait_recv()

    kv_copies = [kv_copy(j, to) for j, to in enumerate(peers)]
    for copy in kv_copies:
        copy.start()
    kv_all[side, z, chip, core] = kv_out[c]

    def relay(level, pair, lane, to):
        slot = kv_all.at[side, level, pair]
        return remote(slot, slot, g_send.at[lane, level, pair], g_recv.at[side, level, pair], to)

    def send_along(level, pair, lane, start):
        to_row = (r + 2, r - 2, partner)[lane]
        copy = relay(level, pair, lane, (to_row, c))

        def act():
            copy.start() if start else copy.wait_send()

        if lane == 0:
            pl.when(z + 1 < steps)(act)
        elif lane == 1:
            pl.when(z >= 1)(act)
        else:
            act()

    def chunk(j):
        return lax.rem(chip + j, pairs)

    def own(j, start):
        for lane in range(3):
            send_along(z, chunk(j), lane, start)

    def each(step, j, start):
        for level, there, lane in ((z - step, z - step >= 0, 0), (z + step, z + step < steps, 1)):

            @pl.when(there)
            def _():
                if start:
                    relay(level, chunk(j), lane, (partner, c)).wait_recv()
                send_along(level, chunk(j), lane, start)
                send_along(level, chunk(j), 2, start)

    q_proj[1] = project(x_halo, 0)
    kv_wait(nc - 2, peers[nc - 2])
    own(0, True)

    parts = [
        pooled(q_proj, pool_q, slice(0, width), 2 * p, 2 * q) for p in range(2) for q in range(2)
    ]
    mixed_order = jnp.concatenate(parts, axis=0)
    count = 4 * per
    t = lax.broadcasted_iota(jnp.int32, (count, 1), 0)
    q_row = t // (cols // 2)
    q_col = t - q_row * (cols // 2)
    which = 2 * lax.rem(q_row, 2) + lax.rem(q_col, 2)
    src = which * per + (q_row // 2) * (cols // 4) + q_col // 2
    lanes = lax.broadcasted_iota(jnp.int32, (count, count), 1)
    order = jnp.where(lanes == src, 1.0, 0.0).astype(jnp.bfloat16)
    natural = dot32(order, mixed_order).astype(jnp.bfloat16)
    wide = q_out.shape[2]
    for g in range(nc):
        piece_q = natural[:, g * group : (g + 1) * group]
        q_out[g] = jnp.concatenate(
            [piece_q, jnp.zeros((count, wide - group), jnp.bfloat16)], axis=1
        )

    def q_copy(j, to):
        return remote(q_out.at[to], q_in.at[c], q_send.at[j], q_recv.at[c], (r, to))

    q_copies = [q_copy(j, to) for j, to in enumerate(peers)]
    for copy in q_copies:
        copy.start()
    q_in[c] = q_out[c]

    for j in range(nc - 2):
        kv_wait(j, peers[j])
    for j in range(1, pairs):
        own(j, True)
    keys = nc * per
    factor = float(head) ** (-0.5) * math.log2(math.e)
    kv_lanes = 2 * group
    lane = lax.broadcasted_iota(jnp.int32, (count, wide), 1)
    shift = wide - group
    stack = heads * count

    def stack_queries():
        for j, to in enumerate(peers):
            remote(q_out.at[to], q_in.at[to], q_send.at[j], q_recv.at[to], (r, to)).wait_recv()
        for g in range(nc):
            q = q_in[g]
            for h in range(heads):
                kept = (lane >= h * head) & (lane < (h + 1) * head)
                at = g * stack + h * count
                q_all[at : at + count, :] = jnp.where(kept, q, jnp.zeros_like(q))

    def absorb(from_side, level, first=False):
        k_part = kv_all[from_side, level, :, :, :, 0:wide].reshape(keys, wide)
        v_part = kv_all[from_side, level, :, :, :, kv_lanes - wide : kv_lanes].reshape(keys, wide)
        scores = lax.dot_general(
            k_part, q_all[...], (((1,), (1,)), ((), ())), preferred_element_type=jnp.float32
        )
        high = jnp.max(scores, axis=0, keepdims=True)
        top = high if first else jnp.maximum(peak[...], high)
        expo = jnp.exp2((scores - top) * factor)
        piece_sum = jnp.sum(expo, axis=0, keepdims=True)
        numer = dot32(v_part.T[shift:, :], expo.astype(jnp.bfloat16))
        if first:
            summed[...] = piece_sum
            acc[...] = numer
        else:
            fade = jnp.exp2((peak[...] - top) * factor)
            summed[...] = summed[...] * fade + piece_sum
            acc[...] = acc[...] * fade + numer
        peak[...] = top

    def absorb_both(step, visit):
        def one(k, carry):
            level = z - step + 2 * k * step
            pl.when((level >= 0) & (level < steps))(lambda: visit(level))
            return carry

        lax.fori_loop(0, 2, one, 0)

    for j in range(pairs):
        each(1, j, True)
    stack_queries()
    absorb(side, z, True)

    def own_step(step, carry):
        absorb_both(step, lambda level: absorb(side, level))
        for j in range(pairs):
            each(step + 1, j, True)
        return carry

    lax.fori_loop(1, steps, own_step, 0)

    def from_partner(level):
        for pair in range(pairs):
            slot = kv_all.at[1 - side, level, pair]
            remote(
                slot, slot, g_send.at[2, level, pair], g_recv.at[1 - side, level, pair],
                (partner, c),
            ).wait_recv()
        absorb(1 - side, level)

    def partner_step(k, carry):
        step = (k + 1) // 2
        level = z + step * (2 * lax.rem(k, 2) - 1)
        pl.when((level >= 0) & (level < steps))(lambda: from_partner(level))
        return carry

    lax.fori_loop(0, 2 * steps - 1, partner_step, 0)

    def finish(g):
        lanes_g = pl.ds(pl.multiple_of(g * stack, 128), stack)
        numer = acc[:, lanes_g] / summed[:, lanes_g]
        picked = [
            numer[h * head : (h + 1) * head, h * count : (h + 1) * count] for h in range(heads)
        ]
        att_out[g] = jnp.concatenate(picked, axis=0).astype(jnp.bfloat16)

    def att_copy(j, to):
        return remote(att_out.at[to], att_in.at[c], o_send.at[j], o_recv.at[c], (r, to))

    def second_step(j, carry):
        to = peer(j)
        finish(to)
        att_copy(j, to).start()
        return carry

    lax.fori_loop(0, nc - 1, second_step, 0)
    finish(c)
    att_in[c] = att_out[c]
    for j, to in enumerate(peers):
        remote(att_out.at[to], att_in.at[to], o_send.at[j], o_recv.at[to], (r, to)).wait_recv()
    for g in range(nc):
        out[g * group : (g + 1) * group, :] = att_in[g]

    pl.when(r < nr - 1)(lambda: row_copy.wait_send())
    pl.when(c < nc - 1)(lambda: col_copy.wait_send())
    pl.when((r < nr - 1) & (c < nc - 1))(lambda: cor_copy.wait_send())
    for copy in kv_copies + q_copies:
        copy.wait_send()
    for j, to in enumerate(peers):
        att_copy(j, to).wait_send()
    for j in range(pairs):
        own(j, False)
    for step in range(1, steps):
        for j in range(pairs):
            each(step, j, False)


def mix_kernel(attended, w_out, out):
    mixed = lax.dot_general(
        attended[...], w_out[...], (((0,), (0,)), ((), ())), preferred_element_type=jnp.float32
    )
    out[...] = mixed.astype(jnp.bfloat16)


def by_kernel(nr, nc, patches, norm_gain, w_qkv, pool_q, pool_kv, w_out):
    rows, cols, width = patches.shape
    per = (rows // 4) * (cols // 4)
    count = 4 * per
    group = width // nc
    heads = HEADS // nc
    wide = -(-group // 128) * 128
    total = rows * cols + rows + 2 * cols
    total = -(-total // 16) * 16
    steps, pairs = nr // 2, nc // 2
    bf16, f32 = jnp.bfloat16, jnp.float32
    dma = pltpu.SemaphoreType.DMA
    vmem = pl.BlockSpec(memory_space=pltpu.VMEM)
    attended = pl.pallas_call(
        functools.partial(section_kernel, nr, nc),
        out_shape=jax.ShapeDtypeStruct((width, count), bf16),
        in_specs=[vmem, vmem, pl.BlockSpec(memory_space=pl.ANY), vmem, vmem],
        out_specs=vmem,
        scratch_shapes=[
            pltpu.VMEM((total, width), bf16),
            pltpu.VMEM((rows, width), bf16),
            pltpu.VMEM((rows, width), bf16),
            pltpu.VMEM((cols, width), bf16),
            pltpu.VMEM((cols, width), bf16),
            pltpu.VMEM((nc, per, 2 * group), bf16),
            pltpu.VMEM((2, steps, pairs, 2, per, 2 * group), bf16),
            pltpu.VMEM((nc, count, wide), bf16),
            pltpu.VMEM((nc, count, wide), bf16),
            pltpu.VMEM((nc, group, count), bf16),
            pltpu.VMEM((nc, group, count), bf16),
            pltpu.VMEM(w_qkv.shape, bf16),
            pltpu.VMEM((nc * heads * count, wide), bf16),
            pltpu.VMEM((group, nc * heads * count), f32),
            pltpu.VMEM((1, nc * heads * count), f32),
            pltpu.VMEM((1, nc * heads * count), f32),
            dma((3,)),
            dma((3,)), dma((3,)),
            dma((nc,)), dma((nc,)),
            dma((3, steps, pairs)), dma((2, steps, pairs)),
            dma((nc,)), dma((nc,)),
            dma((nc,)), dma((nc,)),
        ],
        compiler_params=pltpu.CompilerParams(
            collective_id=0, has_side_effects=True, vmem_limit_bytes=56 * 1024 * 1024
        ),
    )(patches, norm_gain, w_qkv, pool_q, pool_kv)
    mixed = pl.pallas_call(
        mix_kernel,
        out_shape=jax.ShapeDtypeStruct((count, width), bf16),
        in_specs=[vmem, vmem],
        out_specs=vmem,
        compiler_params=pltpu.CompilerParams(vmem_limit_bytes=8 * 1024 * 1024),
    )(attended, w_out)
    return mixed.reshape(rows // 2, cols // 2, width)


def solution(mesh):
    nr, nc = mesh.shape["row"], mesh.shape["col"]
    placed = (P("row", "col", None), P(), P(), P(), P(), P())
    fits = nr % 2 == 0 and nc % 2 == 0 and HEADS % nc == 0
    body = functools.partial(by_kernel, nr, nc) if fits else on_device
    return jax.shard_map(
        body, mesh=mesh, in_specs=placed, out_specs=P("row", "col", None), check_vma=False
    )
```
